32 devices in a mesh: seq: 16 (over z, y, core), head: 2 (over x).
Axes of the slice: x: 2, y: 2, z: 4, core: 2. Of those that a mesh axis runs over, the one named last changes fastest.
Arguments:
- queries: bfloat16 [4096, 4096], P('seq', 'head'), may hold values from -8 to 8
- key_rows: bfloat16 [4096, 4096], P('seq', 'head'), may hold values from -8 to 8
- value_rows: bfloat16 [4096, 4096], P('seq', 'head'), may hold values from -12 to 12
- stream: bfloat16 [4096, 4096], P('seq', 'head'), may hold values from -6 to 11
- norm_gain: float32 [4096], P('head'), may hold values from 0.5 to 1.5
- norm_bias: float32 [4096], P('head'), may hold values from -3 to 3
- head_offsets: int32 [4, 32], replicated, may hold values from 0 to 15, as said below
- cotangent: bfloat16 [4096, 4096], P('seq', 'head'), may hold values from -24 to 24
Outputs:
- normed_out: bfloat16 [4096, 4096], P('seq', 'head')
- grad_queries: float32 [4096, 4096], P('seq', 'head')
- grad_keys: float32 [4096, 4096], P('seq', 'head')
- grad_values: float32 [4096, 4096], P('seq', 'head')
The draws below stay inside these ranges and needn't reach their ends.
Inputs may be any that keep to these rules, and one draw needn't show every extreme that they name: `head_offsets`: row b - 1 holds the offsets of branch b; each value 0 to 2 ** b - 1 is the offset of exactly 32 / 2 ** b heads of that row.
All inputs are finite; a program needn't handle non-finite values.
Results may differ from the reference program's by a relative error of at most 0.0055.
Values may be sent and summed in bfloat16 or wider, within the bound.
No kernel may reach another device: no remote copies, remote signals or barrier semaphores. Data moves between devices by JAX's collectives and lax.ppermute only.
A program may use at most 192 MiB of HBM per device.

```python
import jax
import jax.numpy as jnp
from jax import lax

HEADS = 32
HEAD_DIM = 128
SHARD_TOK = 256
BRANCHES = 4
WIDTH = 4096
TOKENS = 4096


def draw_queries(key, part):
    inner = jax.random.fold_in(key, 11)
    drawn = jnp.clip(1.5 * jax.random.normal(inner, (TOKENS, WIDTH), jnp.float32), -6.0, 6.0)
    return drawn.astype(jnp.bfloat16)


def draw_key_rows(key, part):
    inner = jax.random.fold_in(key, 23)
    drawn = jnp.clip(1.5 * jax.random.normal(inner, (TOKENS, WIDTH), jnp.float32), -6.0, 6.0)
    return drawn.astype(jnp.bfloat16)


def draw_stream(key, part):
    column = jnp.arange(WIDTH, dtype=jnp.float32) / (WIDTH - 1)
    inner = jax.random.fold_in(key, 31)
    col_scale = 0.5 * jnp.power(3.0, column)
    drawn = (jnp.clip(jax.random.normal(inner, (TOKENS, WIDTH), jnp.float32), -4.0, 4.0) + 0.5) * col_scale[None, :]
    return drawn.astype(jnp.bfloat16)


def draw_head_offsets(key, part):
    rows_list = []
    for branch_row in range(BRANCHES):
        order = jax.random.permutation(jax.random.fold_in(key, 41 + branch_row), HEADS).astype(jnp.int32)
        rows_list.append(order % 2 ** (branch_row + 1))
    return jnp.stack(rows_list).astype(jnp.int32)


def levels(stream_key, extent, cuts, low, top_value):
    level = 1.0
    for dim, shards_of in cuts:
        draws = jax.random.uniform(jax.random.fold_in(jax.random.fold_in(stream_key, 6), dim), (shards_of,), jnp.float32, low / len(cuts), top_value / len(cuts))
        level = level * jnp.repeat(jnp.exp(draws), extent[dim] // shards_of).reshape((-1,) + (1,) * (len(extent) - 1 - dim))
    return level


def normal_values(key, shape, width, most, cuts=(), held_as=jnp.bfloat16):
    values = jax.random.normal(key, shape, jnp.float32) * width
    if len(cuts) > 0:
        values = levels(key, shape, cuts, -0.22, 0.18) * values
    return jnp.clip(values, min=-most, max=most).astype(held_as)


def setup_inputs(seed: int = 0) -> dict:
    arg_keys = jax.random.split(jax.random.key(seed), 9)
    return {
        "queries": draw_queries(jax.random.fold_in(arg_keys[8], 71), 0),
        "key_rows": draw_key_rows(jax.random.fold_in(arg_keys[8], 71), 0),
        "value_rows": normal_values(arg_keys[2], (TOKENS, WIDTH), 2.0, 12.0, ((0, 16), (1, 2))),
        "stream": draw_stream(jax.random.fold_in(arg_keys[8], 71), 0),
        "norm_gain": jnp.clip(1.0 + 0.1 * jax.random.normal(arg_keys[4], (WIDTH,), jnp.float32), 0.5, 1.5),
        "norm_bias": normal_values(arg_keys[5], (WIDTH,), 0.5, 3.0, ((0, 2),), jnp.float32),
        "head_offsets": draw_head_offsets(jax.random.fold_in(arg_keys[8], 71), 0),
        "cotangent": normal_values(arg_keys[7], (TOKENS, WIDTH), 4.0, 24.0, ((0, 16), (1, 2))),
    }


alpha_res = (2.0 * 24.0) ** 0.25
eps_norm = 1e-05

def pick_rows(source, stride, offsets_now):
    blocks = source.shape[0] // stride
    shaped = source.reshape((blocks, stride) + source.shape[1:])
    chosen = jnp.arange(stride, dtype=jnp.int32)[:, None] == offsets_now[None, :]
    member = chosen.reshape((1, stride, offsets_now.shape[0]) + (1,) * (source.ndim - 2))
    return lax.optimization_barrier(jnp.sum(jnp.where(member, shaped, jnp.zeros((), source.dtype)), axis=1)).astype(source.dtype)

def place_rows(piece_rows, stride, offsets_now, filler):
    chosen = jnp.arange(stride, dtype=jnp.int32)[:, None] == offsets_now[None, :]
    member = chosen.reshape((1, stride, offsets_now.shape[0]) + (1,) * (piece_rows.ndim - 2))
    spread = jnp.where(member, piece_rows[:, None], jnp.asarray(filler, piece_rows.dtype))
    return spread.reshape((piece_rows.shape[0] * stride,) + piece_rows.shape[1:])

def segment_view(source):
    return source.reshape((source.shape[0] // SHARD_TOK, SHARD_TOK) + source.shape[1:])

def flat_view(source):
    return source.reshape((source.shape[0] * source.shape[1],) + source.shape[2:])

def branch_forward(query_rows, key_set, value_set, scaling):
    scores = jnp.einsum('qhe,khe->hqk', query_rows.astype(jnp.float32), key_set.astype(jnp.float32)) * scaling
    maxima = lax.optimization_barrier(jnp.max(scores, axis=2))
    weights = jnp.exp(scores - maxima[:, :, None])
    totals = lax.optimization_barrier(jnp.sum(weights, axis=2))
    rounded = lax.optimization_barrier(weights.astype(jnp.bfloat16)).astype(jnp.float32)
    blended = jnp.einsum('hqk,khe->qhe', rounded, value_set.astype(jnp.float32))
    return (blended / totals.T[:, :, None], maxima.T, totals.T)

def branch_backward(grouped, scaling):
    query_rows, grad_rows, lse_rows, delta_rows, key_set, value_set = grouped
    grad_wide = grad_rows.astype(jnp.float32)
    scores = jnp.einsum('qhe,khe->hqk', query_rows.astype(jnp.float32), key_set.astype(jnp.float32)) * scaling
    probs = jnp.exp(scores - lse_rows.T[:, :, None])
    rounded = lax.optimization_barrier(probs.astype(jnp.bfloat16)).astype(jnp.float32)
    dvalue = jnp.einsum('hqk,qhe->khe', rounded, grad_wide)
    dprob = jnp.einsum('qhe,khe->hqk', grad_wide, value_set.astype(jnp.float32))
    dscore = lax.optimization_barrier((probs * (dprob - delta_rows.T[:, :, None]) * scaling).astype(jnp.bfloat16)).astype(jnp.float32)
    dquery = jnp.einsum('hqk,khe->qhe', dscore, key_set.astype(jnp.float32))
    dkey = jnp.einsum('hqk,qhe->khe', dscore, query_rows.astype(jnp.float32))
    return (dquery, dkey, dvalue)

def reference(queries, key_rows, value_rows, stream, norm_gain, norm_bias, head_offsets, cotangent):
    scaling = HEAD_DIM ** (-0.5)
    shape_three = (TOKENS, HEADS, HEAD_DIM)
    query_all = queries.reshape(shape_three)
    key_all = key_rows.reshape(shape_three)
    value_all = value_rows.reshape(shape_three)
    offset_list = [jnp.zeros((HEADS,), jnp.int32)] + [head_offsets[branch] for branch in range(BRANCHES)]
    blended_list = []
    maxima_list = []
    totals_list = []
    for branch in range(BRANCHES + 1):
        stride = 2 ** branch
        offsets_now = offset_list[branch]
        grouped = tuple((segment_view(pick_rows(source, stride, offsets_now)) for source in (query_all, key_all, value_all)))
        result = lax.map(lambda triple: branch_forward(triple[0], triple[1], triple[2], scaling), grouped)
        blended_list.append(place_rows(flat_view(result[0]), stride, offsets_now, 0.0))
        maxima_list.append(place_rows(flat_view(result[1]), stride, offsets_now, -jnp.inf))
        totals_list.append(place_rows(flat_view(result[2]), stride, offsets_now, 0.0))
    row_peak = maxima_list[0]
    for maxima in maxima_list[1:]:
        row_peak = jnp.maximum(row_peak, maxima)
    shares = [totals * jnp.exp(maxima - row_peak) for totals, maxima in zip(totals_list, maxima_list)]
    normaliser = shares[0]
    for shares_now in shares[1:]:
        normaliser = normaliser + shares_now
    attention = jnp.zeros(shape_three, jnp.float32)
    for shares_now, blended in zip(shares, blended_list):
        attention = attention + (shares_now / normaliser)[:, :, None] * blended
    pre_norm = alpha_res * stream.astype(jnp.float32) + attention.reshape(TOKENS, WIDTH)
    centre = lax.optimization_barrier(jnp.mean(pre_norm, axis=1))
    centred = pre_norm - centre[:, None]
    inv_std = 1.0 / jnp.sqrt(lax.optimization_barrier(jnp.mean(centred * centred, axis=1)) + eps_norm)
    normed = centred * inv_std[:, None]
    normed_out = (norm_gain * normed + norm_bias).astype(jnp.bfloat16)
    grad_norm = cotangent.astype(jnp.float32) * norm_gain
    mean_grad = lax.optimization_barrier(jnp.mean(grad_norm, axis=1))
    mean_cross = lax.optimization_barrier(jnp.mean(grad_norm * normed, axis=1))
    grad_pre = inv_std[:, None] * (grad_norm - mean_grad[:, None] - normed * mean_cross[:, None])
    grad_attn = grad_pre.astype(jnp.bfloat16).reshape(shape_three)
    delta_all = lax.optimization_barrier(jnp.sum(grad_attn.astype(jnp.float32) * attention, axis=2))
    lse_all = row_peak + jnp.log(normaliser)
    grad_query = jnp.zeros(shape_three, jnp.float32)
    grad_key = jnp.zeros(shape_three, jnp.float32)
    grad_value = jnp.zeros(shape_three, jnp.float32)
    for branch in range(BRANCHES + 1):
        stride = 2 ** branch
        offsets_now = offset_list[branch]
        grouped = tuple((segment_view(pick_rows(source, stride, offsets_now)) for source in (query_all, grad_attn, lse_all, delta_all, key_all, value_all)))
        result = lax.map(lambda grouped_now: branch_backward(grouped_now, scaling), grouped)
        grad_query = grad_query + place_rows(flat_view(result[0]), stride, offsets_now, 0.0)
        grad_key = grad_key + place_rows(flat_view(result[1]), stride, offsets_now, 0.0)
        grad_value = grad_value + place_rows(flat_view(result[2]), stride, offsets_now, 0.0)
    return (normed_out, grad_query.reshape(TOKENS, WIDTH), grad_key.reshape(TOKENS, WIDTH), grad_value.reshape(TOKENS, WIDTH))
```

```python
import functools
import math

import jax
import jax.numpy as jnp
from jax import lax
from jax.experimental import pallas as pl
from jax.experimental.pallas import tpu as pltpu
from jax.sharding import PartitionSpec as P

HEAD_DIM = 128
BRANCHES = 4
FAR = (2, 3, 4)
STAT_ROWS = 8

alpha_res = (2.0 * 24.0) ** 0.25
eps_norm = 1e-05
scaling = HEAD_DIM ** (-0.5)
scaling2 = scaling * math.log2(math.e)

f32 = jnp.float32
bf16 = jnp.bfloat16


def dot_nt(a, b):
    return lax.dot_general(a, b, (((1,), (1,)), ((), ())), preferred_element_type=f32)


def dot_nn(a, b):
    return lax.dot_general(a, b, (((1,), (0,)), ((), ())), preferred_element_type=f32)


def dot_tn(a, b):
    return lax.dot_general(a, b, (((0,), (0,)), ((), ())), preferred_element_type=f32)


def flip(block, axis, mask):
    count = lax.axis_size(axis)
    return lax.ppermute(block, axis, [(i, i ^ mask) for i in range(count)])


def wide(column_block, times):
    return jnp.concatenate([column_block] * times, axis=1)


def attend(query, key, value):
    scores = dot_nt(query, key)
    peak = jnp.max(scores, axis=1, keepdims=True)
    weights = jnp.exp2((scores - peak) * scaling2).astype(bf16)
    both = dot_nn(weights, jnp.concatenate([value, jnp.ones_like(value)], axis=1))
    total = both[:, HEAD_DIM:]
    return both[:, :HEAD_DIM] / total, peak * scaling2 + jnp.log2(total)


def merged(out_a, lse_a, out_b, lse_b):
    peak = jnp.maximum(lse_a, lse_b)
    part_a = jnp.exp2(lse_a - peak)
    part_b = jnp.exp2(lse_b - peak)
    total = part_a + part_b
    return (out_a * part_a + out_b * part_b) / total, peak + jnp.log2(total)


class Plan:
    def __init__(self, rows, heads_here, meta, offsets):
        self.rows = rows
        self.heads = heads_here // 2
        self.meta = meta
        self.offsets = offsets

    def taken(self, branch):
        return self.rows >> branch

    def own(self):
        heads = self.heads
        return pl.BlockSpec((self.rows, HEAD_DIM), lambda h, meta, off: (0, meta[0] * heads + h))

    def row(self):
        heads = self.heads
        return pl.BlockSpec((1, HEAD_DIM), lambda h, meta, off: (0, meta[0] * heads + h))

    def cols(self, rows):
        return pl.BlockSpec((rows, HEAD_DIM), lambda h, meta, off: (0, h))

    def lead(self, shape):
        n = len(shape)
        block = tuple(shape[:-3]) + (1,) + tuple(shape[-2:])
        return pl.BlockSpec(block, lambda h, meta, off: (0,) * (n - 3) + (h, 0, 0))

    def stack(self, count, rows):
        return pl.BlockSpec((count, rows, HEAD_DIM), lambda h, meta, off: (0, 0, h))

    def call(self, body, ins, in_specs, outs, out_specs, scratch=(), grid=None, flops=0):
        size = sum(x.size * x.dtype.itemsize for x in ins) + sum(
            math.prod(o.shape) * jnp.dtype(o.dtype).itemsize for o in outs
        )
        return pl.pallas_call(
            body,
            out_shape=outs,
            grid_spec=pltpu.PrefetchScalarGridSpec(
                num_scalar_prefetch=2,
                grid=grid or (self.heads,),
                in_specs=in_specs,
                out_specs=out_specs,
                scratch_shapes=list(scratch),
            ),
            compiler_params=pltpu.CompilerParams(dimension_semantics=("arbitrary",)),
            cost_estimate=pl.CostEstimate(flops=flops, bytes_accessed=size, transcendentals=0),
        )(self.meta, self.offsets, *ins)


def head_offset(meta, off, heads, branch, h):
    return off[branch - 1, meta[1] + meta[0] * heads + h]


def pick_body(plan, count, meta, off, *refs):
    ins, outs, scratch = refs[: 2 * count], refs[2 * count : 2 * count + 3], refs[-1]
    h = pl.program_id(0)
    for i in range(2 * count):
        scratch[i] = ins[i][...].astype(f32)
    for branch, out in zip(FAR, outs):
        taken = plan.taken(branch)
        start = head_offset(meta, off, plan.heads, branch, h)
        for i in range(2 * count):
            rows = scratch[i, pl.ds(start, taken, stride=2**branch), :]
            out[0, i // 2, 0, (i % 2) * taken : (i % 2 + 1) * taken, :] = rows.astype(bf16)


def pick(plan, pairs):
    count = len(pairs)
    ins = [x for pair in pairs for x in pair]
    specs = [plan.own(), plan.cols(plan.rows)] * count
    outs = [
        jax.ShapeDtypeStruct((1, count, plan.heads, 2 * plan.taken(b), HEAD_DIM), bf16) for b in FAR
    ]
    return plan.call(
        functools.partial(pick_body, plan, count),
        ins,
        specs,
        outs,
        [plan.lead(o.shape) for o in outs],
        [pltpu.VMEM((2 * count, plan.rows, HEAD_DIM), f32)],
    )


def near_forward_body(plan, meta, off, qo, qr, ko, kr, vo, vr, out, lse, scratch):
    h = pl.program_id(0)
    rows, taken = plan.rows, plan.taken(1)
    start = head_offset(meta, off, plan.heads, 1, h)
    for i, ref in enumerate((qo, qr, ko, kr, vo, vr)):
        scratch[i] = ref[...].astype(f32)
    for seg, (q, k, v) in enumerate(((qo, ko, vo), (qr, kr, vr))):
        o, l2 = attend(q[...], k[...], v[...])
        out[seg * rows : (seg + 1) * rows, :] = o
        lse[0, seg * rows : (seg + 1) * rows, :] = l2

    def member(i):
        return jnp.concatenate(
            [scratch[i + s, pl.ds(start, taken, stride=2), :] for s in range(2)], axis=0
        ).astype(bf16)

    o, l2 = attend(member(0), member(2), member(4))
    for seg in range(2):
        where = pl.ds(seg * rows + start, taken, stride=2)
        part = slice(seg * taken, (seg + 1) * taken)
        new_o, new_l = merged(out[where, :], lse[0, where, :], o[part], l2[part])
        out[where, :] = new_o
        lse[0, where, :] = new_l


def near_forward(plan, q, k, v):
    rows, heads = plan.rows, plan.heads
    outs = [
        jax.ShapeDtypeStruct((2 * rows, heads * HEAD_DIM), f32),
        jax.ShapeDtypeStruct((heads, 2 * rows, HEAD_DIM), f32),
    ]
    return plan.call(
        functools.partial(near_forward_body, plan),
        [*q, *k, *v],
        [plan.own(), plan.cols(rows)] * 3,
        outs,
        [plan.cols(2 * rows), plan.lead(outs[1].shape)],
        [pltpu.VMEM((6, rows, HEAD_DIM), f32)],
        flops=heads * 3 * 4 * rows * rows * HEAD_DIM,
    )


def gathered(refs, which):
    parts = []
    for ref in refs:
        for n in range(ref.shape[0]):
            parts.append(ref[n, which, 0])
    return jnp.concatenate(parts, axis=0)


def far_forward_body(meta, off, q, *refs):
    pieces, out, lse = refs[:-2], refs[-2], refs[-1]
    o, l2 = attend(q[0, 0, 0], gathered(pieces, 0), gathered(pieces, 1))
    out[0] = o
    lse[0] = l2


def far_forward(plan, branch, q, pieces):
    rows, heads = 2 * plan.taken(branch), plan.heads
    outs = [jax.ShapeDtypeStruct((heads, rows, HEAD_DIM), f32)] * 2
    return plan.call(
        far_forward_body,
        [q, *pieces],
        [plan.lead(q.shape)] + [plan.lead(p.shape) for p in pieces],
        outs,
        [plan.lead(o.shape) for o in outs],
        flops=heads * 4 * rows * plan.rows * HEAD_DIM,
    )


def combine_body(plan, meta, off, *refs):
    near_o, near_l, far, (so, sr, co, cr, gain) = refs[0], refs[1], refs[2:8], refs[8:13]
    attn, lse, stats, pre_all, g_all = refs[13:]
    h = pl.program_id(0)
    rows, heads = plan.rows, plan.heads
    attn[...] = near_o[...]
    lse[...] = near_l[...]
    for i, branch in enumerate(FAR):
        taken = plan.taken(branch)
        start = head_offset(meta, off, heads, branch, h)
        for seg in range(2):
            where = pl.ds(seg * rows + start, taken, stride=2**branch)
            part = slice(seg * taken, (seg + 1) * taken)
            new_o, new_l = merged(
                attn[where, :], lse[0, where, :], far[2 * i][0, part], far[2 * i + 1][0, part]
            )
            attn[where, :] = new_o
            lse[0, where, :] = new_l
    for seg, (s, c) in enumerate(((so, co), (sr, cr))):
        part = slice(seg * rows, (seg + 1) * rows)
        pre_all[h, part, :] = alpha_res * s[...].astype(f32) + attn[part, :]
        g_all[h, part, :] = c[...].astype(f32) * gain[...]

    @pl.when(h == heads - 1)
    def _():
        def total(i, acc):
            return acc + pre_all[i]

        zero = jnp.zeros((2 * rows, HEAD_DIM), f32)
        pre_sum = jnp.sum(lax.fori_loop(0, heads, total, zero), axis=1, keepdims=True)
        centre = pre_sum / (heads * HEAD_DIM)

        def moments(i, acc):
            diff = pre_all[i] - centre
            g = g_all[i]
            return acc[0] + diff * diff, acc[1] + g, acc[2] + g * diff

        sums = lax.fori_loop(0, heads, moments, (zero, zero, zero))
        lane = lax.broadcasted_iota(jnp.int32, (2 * rows, HEAD_DIM), 1)
        table = jnp.broadcast_to(pre_sum, (2 * rows, HEAD_DIM))
        for i in range(3):
            table = jnp.where(lane == i + 1, jnp.sum(sums[i], axis=1, keepdims=True), table)
        stats[...] = jnp.transpose(table)[:STAT_ROWS]


def combine(plan, near, far, stream, cot, gain):
    rows, heads = plan.rows, plan.heads
    outs = [
        jax.ShapeDtypeStruct((2 * rows, heads * HEAD_DIM), f32),
        jax.ShapeDtypeStruct((heads, 2 * rows, HEAD_DIM), f32),
        jax.ShapeDtypeStruct((STAT_ROWS, 2 * rows), f32),
    ]
    far_list = [x for pair in far for x in pair]
    return plan.call(
        functools.partial(combine_body, plan),
        [*near, *far_list, *stream, *cot, gain],
        [plan.cols(2 * rows), plan.lead(near[1].shape)]
        + [plan.lead(x.shape) for x in far_list]
        + [plan.own(), plan.cols(rows)] * 2
        + [plan.row()],
        outs,
        [
            plan.cols(2 * rows),
            plan.lead(outs[1].shape),
            pl.BlockSpec((STAT_ROWS, 2 * rows), lambda h, meta, off: (0, 0)),
        ],
        [pltpu.VMEM((heads, 2 * rows, HEAD_DIM), f32)] * 2,
        flops=40 * 2 * rows * heads * HEAD_DIM,
    )


def join_stats(mine, other, count):
    gap = (mine[0] - other[0]) / count
    return jnp.stack(
        [
            mine[0] + other[0],
            mine[1] + other[1] + gap * gap * (count / 2),
            mine[2] + other[2],
            mine[3] + other[3] + gap * 0.5 * (mine[2] - other[2]),
        ]
        + [jnp.zeros_like(mine[0])] * (STAT_ROWS - 4)
    )


def split_rows(lse, delta):
    high = lse.astype(bf16).astype(f32)
    mid = (lse - high).astype(bf16).astype(f32)
    low = lse - high - mid
    delta_high = delta.astype(bf16).astype(f32)
    delta_low = delta - delta_high
    return jnp.concatenate(
        [high, mid, low, delta_high, delta_low] + [jnp.zeros_like(lse)] * (STAT_ROWS - 5), axis=0
    ).astype(bf16)


def norm_body(plan, width, meta, off, *refs):
    stats, attn, lse, so, sr, co, cr, gain, bias = refs[:9]
    no, nr, da_out, delta_out, m2, m3, m4, cols, da_wide = refs[9:]
    h = pl.program_id(0)
    rows, heads = plan.rows, plan.heads

    @pl.when(h == 0)
    def _():
        st = stats[...]
        centre = st[0:1] / width
        inv = 1.0 / jnp.sqrt(st[1:2] / width + eps_norm)
        for i, row in enumerate((centre, inv, st[2:3] / width, st[3:4] * inv / width)):
            cols[i] = jnp.transpose(jnp.broadcast_to(row, (HEAD_DIM, 2 * rows)))

    for seg, (s, c, n) in enumerate(((so, co, no), (sr, cr, nr))):
        part = slice(seg * rows, (seg + 1) * rows)
        att = attn[part, :]
        inv = cols[1, part, :]
        normed = (alpha_res * s[...].astype(f32) + att - cols[0, part, :]) * inv
        n[...] = (gain[...] * normed + bias[...]).astype(bf16)
        g = c[...].astype(f32) * gain[...]
        da = (inv * (g - cols[2, part, :] - normed * cols[3, part, :])).astype(bf16)
        da_out[part, :] = da
        da_f = da.astype(f32)
        da_wide[part, :] = da_f
        delta_out[0, part, :] = jnp.broadcast_to(
            jnp.sum(da_f * att, axis=1, keepdims=True), (rows, HEAD_DIM)
        )
    for branch, msg in zip(FAR, (m2, m3, m4)):
        taken = plan.taken(branch)
        start = head_offset(meta, off, heads, branch, h)
        where = [pl.ds(seg * rows + start, taken, stride=2**branch) for seg in range(2)]
        for seg in range(2):
            msg[0, 0, 0, seg * taken : (seg + 1) * taken, :] = da_wide[where[seg], :].astype(bf16)
        pad = [jnp.zeros((HEAD_DIM - 2 * taken, HEAD_DIM), f32)] if 2 * taken < HEAD_DIM else []

        def as_row(read):
            return jnp.transpose(jnp.concatenate([read(w) for w in where] + pad, axis=0))[0:1]

        msg[0, 0, 0, 2 * taken :, :] = split_rows(
            as_row(lambda w: lse[0, w, :]), as_row(lambda w: delta_out[0, w, :])
        )


def norm(plan, width, stats, attn, lse, stream, cot, gain, bias):
    rows, heads = plan.rows, plan.heads
    sd = jax.ShapeDtypeStruct
    outs = [
        sd((rows, heads * HEAD_DIM), bf16),
        sd((rows, heads * HEAD_DIM), bf16),
        sd((2 * rows, heads * HEAD_DIM), bf16),
        sd((heads, 2 * rows, HEAD_DIM), f32),
    ] + [sd((1, 1, heads, 2 * plan.taken(b) + STAT_ROWS, HEAD_DIM), bf16) for b in FAR]
    return plan.call(
        functools.partial(norm_body, plan, width),
        [stats, attn, lse, *stream, *cot, gain, bias],
        [
            pl.BlockSpec((STAT_ROWS, 2 * rows), lambda h, meta, off: (0, 0)),
            plan.cols(2 * rows),
            plan.lead(lse.shape),
        ]
        + [plan.own(), plan.cols(rows)] * 2
        + [plan.row()] * 2,
        outs,
        [plan.cols(rows), plan.cols(rows), plan.cols(2 * rows)] + [plan.lead(o.shape) for o in outs[3:]],
        [pltpu.VMEM((4, 2 * rows, HEAD_DIM), f32), pltpu.VMEM((2 * rows, HEAD_DIM), f32)],
        flops=40 * 2 * rows * heads * HEAD_DIM,
    )


def dscores(query, key, value, grad, lse, delta):
    reach = key.shape[0] // HEAD_DIM
    probs = jnp.exp2(dot_nt(query, key) * scaling2 - wide(lse, reach))
    dprob = dot_nt(grad, value)
    return probs.astype(bf16), (probs * (dprob - wide(delta, reach))).astype(bf16)


def near_backward_body(plan, counts, meta, off, *refs):
    qo, qr, ko, kr, vo, vr, da, lse, delta = refs[:9]
    pieces = refs[9 : 9 + sum(counts)]
    dq_own, dq_rec, kv_own, kv_rec, scratch, sums = refs[9 + sum(counts) :]
    h = pl.program_id(0)
    rows, heads = plan.rows, plan.heads
    for i, ref in enumerate((qo, qr, ko, kr, vo, vr)):
        scratch[i] = ref[...].astype(f32)
    for seg in range(2):
        scratch[6 + seg] = da[seg * rows : (seg + 1) * rows, :].astype(f32)
    for seg, (q, k, v) in enumerate(((qo, ko, vo), (qr, kr, vr))):
        part = slice(seg * rows, (seg + 1) * rows)
        grad = da[part, :]
        probs, ds = dscores(q[...], k[...], v[...], grad, lse[0, part, :], delta[0, part, :])
        sums[0, part, :] = dot_nn(ds, k[...])
        sums[1, part, :] = dot_tn(ds, q[...])
        sums[2, part, :] = dot_tn(probs, grad)

    def member(i, branch, start):
        taken = plan.taken(branch)
        return jnp.concatenate(
            [scratch[i + s, pl.ds(start, taken, stride=2**branch), :] for s in range(2)], axis=0
        ).astype(bf16)

    for branch in range(1, BRANCHES + 1):
        taken = plan.taken(branch)
        start = head_offset(meta, off, heads, branch, h)
        where = [pl.ds(seg * rows + start, taken, stride=2**branch) for seg in range(2)]
        query, grad = member(0, branch, start), member(6, branch, start)
        lse_rows = jnp.concatenate([lse[0, w, :] for w in where], axis=0)
        delta_rows = jnp.concatenate([delta[0, w, :] for w in where], axis=0)
        if branch == 1:
            key, value = member(2, 1, start), member(4, 1, start)
        else:
            first = sum(counts[: branch - 2])
            mine = pieces[first : first + counts[branch - 2]]
            key, value = gathered(mine, 0), gathered(mine, 1)
        probs, ds = dscores(query, key, value, grad, lse_rows, delta_rows)
        grads = [dot_nn(ds, key)]
        if branch == 1:
            grads += [dot_tn(ds, query), dot_tn(probs, grad)]
        for i, rows_new in enumerate(grads):
            for seg in range(2):
                sums[i, where[seg], :] = (
                    sums[i, where[seg], :] + rows_new[seg * taken : (seg + 1) * taken]
                )
    dq_own[...] = sums[0, :rows, :] * scaling
    dq_rec[...] = (sums[0, rows:, :] * scaling).astype(bf16)
    kv_own[0] = sums[1, :rows, :] * scaling
    kv_own[1] = sums[2, :rows, :]
    kv_rec[0] = (sums[1, rows:, :] * scaling).astype(bf16)
    kv_rec[1] = sums[2, rows:, :].astype(bf16)


def near_backward(plan, q, k, v, da, lse, delta, pieces):
    rows, heads = plan.rows, plan.heads
    sd = jax.ShapeDtypeStruct
    width = heads * HEAD_DIM
    outs = [sd((rows, width), f32), sd((rows, width), bf16), sd((2, rows, width), f32), sd((2, rows, width), bf16)]
    counts = [len(p) for p in pieces]
    flat = [x for p in pieces for x in p]
    return plan.call(
        functools.partial(near_backward_body, plan, counts),
        [*q, *k, *v, da, lse, delta, *flat],
        [plan.own(), plan.cols(rows)] * 3
        + [plan.cols(2 * rows), plan.lead(lse.shape), plan.lead(delta.shape)]
        + [plan.lead(x.shape) for x in flat],
        outs,
        [plan.cols(rows), plan.cols(rows), plan.stack(2, rows), plan.stack(2, rows)],
        [pltpu.VMEM((8, rows, HEAD_DIM), f32), pltpu.VMEM((3, 2 * rows, HEAD_DIM), f32)],
        flops=heads * 5 * 5 * 2 * rows * rows * HEAD_DIM,
    )


def far_backward_body(taken, n_q, meta, off, kv, *refs):
    q_refs, m_refs, own, rec = refs[:n_q], refs[n_q:-2], refs[-2], refs[-1]
    queries = gathered(q_refs, 0)
    grads, halves = [], [None] * (queries.shape[0] // HEAD_DIM)
    place = 0
    for ref in m_refs:
        for n in range(ref.shape[0]):
            grads.append(ref[n, 0, 0, : 2 * taken, :])
            terms = ref[n, 0, 0, 2 * taken :, :].astype(f32)
            half, shift = divmod(place, HEAD_DIM)
            if shift:
                terms = pltpu.roll(terms, shift, 1)
            halves[half] = terms if halves[half] is None else halves[half] + terms
            place += 2 * taken
    grad = jnp.concatenate(grads, axis=0)
    table = jnp.concatenate(halves, axis=1)
    lse = table[0:1] + table[1:2] + table[2:3]
    delta = table[3:4] + table[4:5]
    key, value = kv[0, 0, 0], kv[0, 1, 0]
    probs = jnp.exp2(dot_nt(key, queries) * scaling2 - lse)
    ds = (probs * (dot_nt(value, grad) - delta)).astype(bf16)
    dkey = dot_nn(ds, queries) * scaling
    dvalue = dot_nn(probs.astype(bf16), grad)
    for i, rows in enumerate((dkey, dvalue)):
        own[i, 0] = rows[:taken]
        rec[i, 0] = rows[taken:].astype(bf16)


def far_backward(plan, branch, kv, q_pieces, m_pieces):
    taken, heads = plan.taken(branch), plan.heads
    outs = [
        jax.ShapeDtypeStruct((2, heads, taken, HEAD_DIM), f32),
        jax.ShapeDtypeStruct((2, heads, taken, HEAD_DIM), bf16),
    ]
    ins = [kv, *q_pieces, *m_pieces]
    return plan.call(
        functools.partial(far_backward_body, taken, len(q_pieces)),
        ins,
        [plan.lead(x.shape) for x in ins],
        outs,
        [plan.lead(o.shape) for o in outs],
        flops=heads * 8 * 2 * taken * plan.rows * HEAD_DIM,
    )


def two_phase(plan, rank):
    heads = plan.heads

    def mine(i):
        return jnp.minimum(i, heads - 1)

    def other(i):
        return jnp.maximum(i - heads, 0)

    def target(i, meta):
        first = i < heads
        return jnp.where(first, meta[0] * heads + i, (1 - meta[0]) * heads + i - heads)

    return mine, other, target


def assemble_q_body(heads, meta, off, dq_own, dq_got, n_own, n_got, dq, normed):
    i = pl.program_id(0)

    @pl.when(i < heads)
    def _():
        dq[...] = dq_own[...]
        normed[...] = n_own[...]

    @pl.when(i >= heads)
    def _():
        dq[...] = dq_got[...].astype(f32)
        normed[...] = n_got[...]


def assemble_q(plan, dq_own, dq_got, n_own, n_got):
    rows, heads = plan.rows, plan.heads
    mine, other, target = two_phase(plan, 2)
    own = pl.BlockSpec((rows, HEAD_DIM), lambda i, meta, off: (0, mine(i)))
    got = pl.BlockSpec((rows, HEAD_DIM), lambda i, meta, off: (0, other(i)))
    out = pl.BlockSpec((rows, HEAD_DIM), lambda i, meta, off: (0, target(i, meta)))
    full = (rows, 2 * heads * HEAD_DIM)
    return plan.call(
        functools.partial(assemble_q_body, heads),
        [dq_own, dq_got, n_own, n_got],
        [own, got, own, got],
        [jax.ShapeDtypeStruct(full, f32), jax.ShapeDtypeStruct(full, bf16)],
        [out, out],
        grid=(2 * heads,),
    )


def assemble_kv_body(plan, meta, off, *refs):
    base, rows_refs, (dk, dv) = refs[:2], refs[2:8], refs[8:]
    heads = plan.heads
    i = pl.program_id(0)
    local = jnp.where(i < heads, meta[0] * heads + i, (1 - meta[0]) * heads + i - heads)

    def fill(which):
        for t, out in enumerate((dk, dv)):
            out[...] = base[which][t].astype(f32)
            for j, branch in enumerate(FAR):
                start = off[branch - 1, meta[1] + local]
                where = pl.ds(start, plan.taken(branch), stride=2**branch)
                out[where, :] = out[where, :] + rows_refs[2 * j + which][t, 0].astype(f32)

    @pl.when(i < heads)
    def _():
        fill(0)

    @pl.when(i >= heads)
    def _():
        fill(1)


def assemble_kv(plan, base_own, base_got, rows_pairs):
    rows, heads = plan.rows, plan.heads
    mine, other, target = two_phase(plan, 2)
    specs = [
        pl.BlockSpec((2, rows, HEAD_DIM), lambda i, meta, off: (0, 0, mine(i))),
        pl.BlockSpec((2, rows, HEAD_DIM), lambda i, meta, off: (0, 0, other(i))),
    ]
    for branch in FAR:
        block = (2, 1, plan.taken(branch), HEAD_DIM)
        specs.append(pl.BlockSpec(block, lambda i, meta, off: (0, mine(i), 0, 0)))
        specs.append(pl.BlockSpec(block, lambda i, meta, off: (0, other(i), 0, 0)))
    out = pl.BlockSpec((rows, HEAD_DIM), lambda i, meta, off: (0, target(i, meta)))
    full = jax.ShapeDtypeStruct((rows, 2 * heads * HEAD_DIM), f32)
    return plan.call(
        functools.partial(assemble_kv_body, plan),
        [base_own, base_got, *[x for pair in rows_pairs for x in pair]],
        specs,
        [full, full],
        [out, out],
        grid=(2 * heads,),
    )


def gather(two, three, four):
    three_y = flip(three, "seq", 2)
    four_far = flip(four, "seq", 8)
    two_y = flip(two, "seq", 2)
    three_z = flip(jnp.concatenate([three, three_y]), "seq", 4)
    four_y = flip(jnp.concatenate([four, four_far]), "seq", 2)
    four_z = flip(jnp.concatenate([four, four_far, four_y]), "seq", 4)
    return [two, two_y], [three, three_y, three_z], [four, four_far, four_y, four_z]


def shards(queries, key_rows, value_rows, stream, norm_gain, norm_bias, head_offsets, cotangent):
    rows = queries.shape[0]
    heads_here = queries.shape[1] // HEAD_DIM
    half = queries.shape[1] // 2
    core = lax.axis_index("seq") & 1
    first_head = lax.axis_index("head") * heads_here
    meta = jnp.stack([core, first_head]).astype(jnp.int32)
    plan = Plan(rows, heads_here, meta, head_offsets)

    def with_other_core(block):
        sent = lax.dynamic_slice_in_dim(block, (1 - core) * half, half, 1)
        return block, flip(sent, "seq", 1)

    k, v = with_other_core(key_rows), with_other_core(value_rows)
    q = with_other_core(queries)
    kv_far = pick(plan, [k, v])
    kv_pieces = gather(*kv_far)
    q_far = pick(plan, [q])
    res, cot = with_other_core(stream), with_other_core(cotangent)
    gain, bias = norm_gain[None, :], norm_bias[None, :]

    near = near_forward(plan, q, k, v)
    far = [far_forward(plan, b, q_far[b - 2], kv_pieces[b - 2]) for b in FAR]
    attn, lse, stats = combine(plan, near, far, res, cot, gain)

    q_pieces = gather(*q_far)

    other = flip(stats, "seq", 1)
    stats = join_stats(stats, jnp.concatenate([other[:, rows:], other[:, :rows]], 1), half)
    width = 2 * half
    mask = 1
    while mask < lax.axis_size("head"):
        stats = join_stats(stats, flip(stats, "head", mask), width)
        width = 2 * width
        mask = 2 * mask
    n_own, n_send, da, delta, *msgs = norm(plan, width, stats, attn, lse, res, cot, gain, bias)
    m_pieces = gather(*msgs)

    dq_own, dq_send, kv_own, kv_send = near_backward(plan, q, k, v, da, lse, delta, kv_pieces)
    grad_query, normed_out = assemble_q(
        plan, dq_own, flip(dq_send, "seq", 1), n_own, flip(n_send, "seq", 1)
    )
    pairs = []
    for b in FAR:
        own, sent = far_backward(plan, b, kv_far[b - 2], q_pieces[b - 2], m_pieces[b - 2])
        pairs.append((own, flip(sent, "seq", 1)))
    grad_key, grad_value = assemble_kv(plan, kv_own, flip(kv_send, "seq", 1), pairs)
    return normed_out, grad_query, grad_key, grad_value


def solution(mesh):
    return jax.shard_map(
        shards,
        mesh=mesh,
        in_specs=(
            P("seq", "head"),
            P("seq", "head"),
            P("seq", "head"),
            P("seq", "head"),
            P("head"),
            P("head"),
            P(),
            P("seq", "head"),
        ),
        out_specs=(P("seq", "head"), P("seq", "head"), P("seq", "head"), P("seq", "head")),
        check_vma=False,
    )
```

```python
import functools
import math
from typing import NamedTuple

import jax
import jax.numpy as jnp
from jax import lax
from jax.experimental import pallas as pl
from jax.experimental.pallas import tpu as pltpu
from jax.sharding import PartitionSpec as P

HEAD_DIM = 128
BRANCHES = 4
FAR = (2, 3, 4)
STAT_ROWS = 8

alpha_res = (2.0 * 24.0) ** 0.25
eps_norm = 1e-05
scaling = HEAD_DIM ** (-0.5)
scaling2 = scaling * math.log2(math.e)

f32 = jnp.float32
bf16 = jnp.bfloat16


def dot_nt(a, b):
    return lax.dot_general(a, b, (((1,), (1,)), ((), ())), preferred_element_type=f32)


def dot_nn(a, b):
    return lax.dot_general(a, b, (((1,), (0,)), ((), ())), preferred_element_type=f32)


def dot_tn(a, b):
    return lax.dot_general(a, b, (((0,), (0,)), ((), ())), preferred_element_type=f32)


def flip(block, axis, mask):
    count = lax.axis_size(axis)
    return lax.ppermute(block, axis, [(i, i ^ mask) for i in range(count)])


def wide(column_block, times):
    return jnp.concatenate([column_block] * times, axis=1)


def attend(query, key, value):
    scores = dot_nt(query, key)
    peak = jnp.max(scores, axis=1, keepdims=True)
    weights = jnp.exp2((scores - peak) * scaling2).astype(bf16)
    both = dot_nn(weights, jnp.concatenate([value, jnp.ones_like(value)], axis=1))
    total = both[:, HEAD_DIM:]
    return both[:, :HEAD_DIM] / total, peak * scaling2 + jnp.log2(total)


def merged(out_a, lse_a, out_b, lse_b):
    peak = jnp.maximum(lse_a, lse_b)
    part_a = jnp.exp2(lse_a - peak)
    part_b = jnp.exp2(lse_b - peak)
    total = part_a + part_b
    return (out_a * part_a + out_b * part_b) / total, peak + jnp.log2(total)


def room(scratch):
    arrays = [x for x in scratch if not isinstance(x, pltpu.SemaphoreType) and hasattr(x, "memory_space")]
    arrays = [x for x in arrays if x.memory_space == pltpu.VMEM]
    return sum(math.prod(x.shape) * jnp.dtype(x.dtype).itemsize for x in arrays) + 4 * 2**20


class Plan:
    def __init__(self, rows, heads_here, meta, offsets):
        self.rows = rows
        self.heads = heads_here // 2
        self.width = self.heads * HEAD_DIM
        self.meta = meta
        self.offsets = offsets

    def taken(self, branch):
        return self.rows >> branch

    def call(
        self,
        body,
        ins,
        outs,
        scratch=(),
        name=None,
        in_place=pltpu.VMEM,
        out_place=pltpu.VMEM,
        aliases=None,
        wait_for=(),
    ):
        given, waited = 2 + len(ins), len(wait_for)

        def without_waited(*refs):
            body(*refs[:given], *refs[given + waited :])

        scalars = pl.BlockSpec(memory_space=pltpu.SMEM)
        return pl.pallas_call(
            without_waited if waited else body,
            out_shape=outs,
            in_specs=[scalars, scalars]
            + [pl.BlockSpec(memory_space=in_place)] * len(ins)
            + [pl.BlockSpec(memory_space=pl.ANY)] * waited,
            out_specs=[
                pl.BlockSpec(memory_space=out_place[i] if isinstance(out_place, list) else out_place)
                for i in range(len(outs))
            ],
            scratch_shapes=list(scratch),
            compiler_params=pltpu.CompilerParams(vmem_limit_bytes=room(scratch)),
            cost_estimate=pl.CostEstimate(flops=0, bytes_accessed=0, transcendentals=0),
            input_output_aliases=aliases or {},
            name=name,
        )(self.meta, self.offsets, *ins, *wait_for)

    def each_head(self, together, body):
        together = min(together, self.heads)
        if together == self.heads:
            for h in range(self.heads):
                body(h, h)
            return

        def step(i, carry):
            for slot in range(together):
                body(i * together + slot, slot)
            return carry

        lax.fori_loop(0, self.heads // together, step, 0)


def lanes(h):
    if isinstance(h, int):
        return slice(h * HEAD_DIM, (h + 1) * HEAD_DIM)
    return pl.ds(pl.multiple_of(h * HEAD_DIM, HEAD_DIM), HEAD_DIM)


def own_lanes(meta, heads, h):
    return pl.ds(pl.multiple_of((meta[0] * heads + h) * HEAD_DIM, HEAD_DIM), HEAD_DIM)


def member_rows(meta, off, heads, branch, h, taken, shift=0):
    start = off[branch - 1, meta[1] + meta[0] * heads + h]
    return pl.ds(start + shift, taken, stride=2**branch)


def halves_body(plan, count, meta, off, *refs):
    ins, out, sems = refs[:count], refs[count], refs[count + 1]
    other = pl.ds(pl.multiple_of((1 - meta[0]) * plan.width, plan.width), plan.width)
    copies = [pltpu.make_async_copy(ref.at[:, other], out.at[i], sems.at[i]) for i, ref in enumerate(ins)]
    for copy in copies:
        copy.start()
    for copy in copies:
        copy.wait()


def halves(plan, blocks):
    count = len(blocks)
    out = jax.ShapeDtypeStruct((count, plan.rows, plan.width), blocks[0].dtype)
    return plan.call(
        functools.partial(halves_body, plan, count),
        [pltpu.with_memory_space_constraint(x, pltpu.HBM) for x in blocks],
        [out],
        [pltpu.SemaphoreType.DMA((count,))],
        name="halves",
        in_place=pltpu.HBM,
    )[0]


def pick_body(plan, count, first, meta, off, *refs):
    owns, got, outs, scratch = refs[:count], refs[count], refs[count + 1 : count + 4], refs[-1]
    heads, rows = plan.heads, plan.rows

    def one(h, slot):
        for i in range(count):
            scratch[slot, 2 * i] = owns[i][:, own_lanes(meta, heads, h)].astype(f32)
            scratch[slot, 2 * i + 1] = got[first + i, :, lanes(h)].astype(f32)
        for branch, out in zip(FAR, outs):
            taken = plan.taken(branch)
            where = member_rows(meta, off, heads, branch, h, taken)
            for i in range(count):
                picked = [scratch[slot, 2 * i + seg, where, :] for seg in range(2)]
                out[0, i, h] = jnp.concatenate(picked, axis=0).astype(bf16)

    plan.each_head(4, one)


def pick(plan, owns, got, first):
    count = len(owns)
    outs = [
        jax.ShapeDtypeStruct((1, count, plan.heads, 2 * plan.taken(b), HEAD_DIM), bf16) for b in FAR
    ]
    return plan.call(
        functools.partial(pick_body, plan, count, first),
        [*owns, got],
        outs,
        [pltpu.VMEM((4, 2 * count, plan.rows, HEAD_DIM), f32)],
        name="pick",
    )


def near_forward_body(plan, together, meta, off, qo, ko, vo, kv_got, q_got, out, lse, wide_in, acc, acc_l):
    heads, rows, taken = plan.heads, plan.rows, plan.taken(1)

    def one(h, slot):
        mine = own_lanes(meta, heads, h)
        seg_in = (
            (qo[:, mine], ko[:, mine], vo[:, mine]),
            (q_got[0, :, lanes(h)], kv_got[0, :, lanes(h)], kv_got[1, :, lanes(h)]),
        )
        for seg in range(2):
            for i in range(3):
                wide_in[slot, 2 * i + seg] = seg_in[seg][i].astype(f32)
        where = member_rows(meta, off, heads, 1, h, taken)
        near = []
        for i in range(3):
            picked = [wide_in[slot, 2 * i + seg, where, :] for seg in range(2)]
            near.append(jnp.concatenate(picked, axis=0).astype(bf16))
        for seg in range(2):
            o, l2 = attend(*seg_in[seg])
            acc[slot, seg] = o
            acc_l[slot, seg] = l2
        o, l2 = attend(*near)
        for seg in range(2):
            part = slice(seg * taken, (seg + 1) * taken)
            new_o, new_l = merged(
                acc[slot, seg, where, :], acc_l[slot, seg, where, :], o[part], l2[part]
            )
            acc[slot, seg, where, :] = new_o
            acc_l[slot, seg, where, :] = new_l
        for seg in range(2):
            part = slice(seg * rows, (seg + 1) * rows)
            out[h, part, :] = acc[slot, seg]
            lse[h, part, :] = acc_l[slot, seg]

    plan.each_head(together, one)


def near_forward(plan, q, k, v, kv_got, q_got):
    rows, heads = plan.rows, plan.heads
    together = 2
    out = jax.ShapeDtypeStruct((heads, 2 * rows, HEAD_DIM), f32)
    pair = pltpu.VMEM((together, 2, rows, HEAD_DIM), f32)
    return plan.call(
        functools.partial(near_forward_body, plan, together),
        [q, k, v, kv_got, q_got],
        [out, out],
        [pltpu.VMEM((together, 6, rows, HEAD_DIM), f32), pair, pair],
        name="near_forward",
    )


class Rows(NamedTuple):
    array: jax.Array
    start: int
    count: int


def whole_rows(array):
    return Rows(array, 0, array.shape[3])


def extents(pieces):
    return [(p.array.shape[0], p.start, p.count) for p in pieces]


def gathered(refs, layout, which, h):
    parts = []
    for ref, (many, start, count) in zip(refs, layout, strict=True):
        for n in range(many):
            parts.append(ref[n, which, h, start : start + count, :])
    return jnp.concatenate(parts, axis=0)


def far_forward_body(plan, layout, meta, off, q, *refs):
    pieces, out, lse = refs[:-2], refs[-2], refs[-1]

    def one(h, slot):
        o, l2 = attend(q[0, 0, h], gathered(pieces, layout, 0, h), gathered(pieces, layout, 1, h))
        out[h] = o
        lse[h] = l2

    plan.each_head(4, one)


def far_forward(plan, branch, q, pieces):
    rows, heads = 2 * plan.taken(branch), plan.heads
    outs = [jax.ShapeDtypeStruct((heads, rows, HEAD_DIM), f32)] * 2
    return plan.call(
        functools.partial(far_forward_body, plan, extents(pieces)),
        [q, *[p.array for p in pieces]],
        outs,
        name=f"far_forward{branch}",
    )


def combine_body(plan, meta, off, *refs):
    near_o, near_l, far, (so, co, sc_got, gain) = refs[0], refs[1], refs[2:8], refs[8:12]
    attn, lse, stats, pre_all, g_all = refs[12:]
    rows, heads = plan.rows, plan.heads

    def one(h, slot):
        mine = own_lanes(meta, heads, h)
        attn[h] = near_o[h]
        lse[h] = near_l[h]
        for i, branch in enumerate(FAR):
            taken = plan.taken(branch)
            for seg in range(2):
                where = member_rows(meta, off, heads, branch, h, taken, seg * rows)
                part = slice(seg * taken, (seg + 1) * taken)
                new_o, new_l = merged(
                    attn[h, where, :], lse[h, where, :], far[2 * i][h, part], far[2 * i + 1][h, part]
                )
                attn[h, where, :] = new_o
                lse[h, where, :] = new_l
        scale = gain[:, mine]
        res = (so[:, mine], sc_got[1, :, lanes(h)])
        cot = (co[:, mine], sc_got[2, :, lanes(h)])
        for seg in range(2):
            part = slice(seg * rows, (seg + 1) * rows)
            pre_all[h, part, :] = alpha_res * res[seg].astype(f32) + attn[h, part, :]
            g_all[h, part, :] = cot[seg].astype(f32) * scale

    plan.each_head(2, one)

    def total(i, acc):
        return acc + pre_all[i]

    for seg in range(2):
        part = slice(seg * rows, (seg + 1) * rows)
        acc = pre_all[0, part, :]
        for i in range(1, heads):
            acc = acc + pre_all[i, part, :]
        pre_sum = jnp.sum(acc, axis=1, keepdims=True)
        centre = pre_sum / (heads * HEAD_DIM)
        second = jnp.zeros((rows, HEAD_DIM), f32)
        g_sum, cross = second, second
        for i in range(heads):
            diff = pre_all[i, part, :] - centre
            g = g_all[i, part, :]
            second, g_sum, cross = second + diff * diff, g_sum + g, cross + g * diff
        lane = lax.broadcasted_iota(jnp.int32, (rows, HEAD_DIM), 1)
        table = jnp.broadcast_to(pre_sum, (rows, HEAD_DIM))
        for i, x in enumerate((second, g_sum, cross)):
            table = jnp.where(lane == i + 1, jnp.sum(x, axis=1, keepdims=True), table)
        stats[:, part] = jnp.transpose(table)[:STAT_ROWS]


def combine(plan, near, far, stream, cot, sc_got, gain):
    rows, heads = plan.rows, plan.heads
    per_head = jax.ShapeDtypeStruct((heads, 2 * rows, HEAD_DIM), f32)
    outs = [per_head, per_head, jax.ShapeDtypeStruct((STAT_ROWS, 2 * rows), f32)]
    return plan.call(
        functools.partial(combine_body, plan),
        [*near, *[x for pair in far for x in pair], stream, cot, sc_got, gain],
        outs,
        [pltpu.VMEM((heads, 2 * rows, HEAD_DIM), f32)] * 2,
        name="combine",
    )


def joined(mine, other, count):
    gap = (mine[0:1] - other[0:1]) / count
    return [
        mine[0:1] + other[0:1],
        mine[1:2] + other[1:2] + gap * gap * (count / 2),
        mine[2:3] + other[2:3],
        mine[3:4] + other[3:4] + gap * 0.5 * (mine[2:3] - other[2:3]),
    ]


def join_body(rows, count, swap, meta, off, mine, other, out):
    theirs = other[...]
    if swap:
        theirs = jnp.concatenate([theirs[:, rows:], theirs[:, :rows]], axis=1)
    for i, row in enumerate(joined(mine[...], theirs, count)):
        out[i : i + 1, :] = row


def join(plan, mine, other, count, swap=False):
    return plan.call(
        functools.partial(join_body, plan.rows, count, swap),
        [mine, other],
        [jax.ShapeDtypeStruct(mine.shape, f32)],
        name="join",
    )[0]


def relay_body(meta, off, three, four, four_far, both, for_z):
    both[0:1] = four[...]
    both[1:2] = four_far[...]
    place = 0
    for ref in (three, four, four_far):
        rows = ref.shape[3]
        for c in range(ref.shape[1]):
            for h in range(ref.shape[2]):
                for_z[0, c, h, place : place + rows, :] = ref[0, c, h]
        place += rows


def relay(plan, three, four, four_far, wait_for):
    _, tensors, heads, rows, width = four.shape
    sd = jax.ShapeDtypeStruct
    outs = [
        sd((2, tensors, heads, rows, width), four.dtype),
        sd((1, tensors, heads, three.shape[3] + 2 * rows, width), four.dtype),
    ]
    return plan.call(relay_body, [three, four, four_far], outs, name="relay", wait_for=wait_for)


def split_rows(lse, delta):
    high = lse.astype(bf16).astype(f32)
    mid = (lse - high).astype(bf16).astype(f32)
    low = lse - high - mid
    delta_high = delta.astype(bf16).astype(f32)
    delta_low = delta - delta_high
    return jnp.concatenate(
        [high, mid, low, delta_high, delta_low] + [jnp.zeros_like(lse)] * (STAT_ROWS - 5), axis=0
    ).astype(bf16)


def norm_body(plan, full_width, together, meta, off, *refs):
    stats, stats_got, attn, lse, so, co, sc_got, gain, bias = refs[:9]
    q_far = refs[9:12]
    n_own, n_send, da_out, delta_out, m2, m3, m4, cols, da_wide, delta_wide = refs[12:]
    rows, heads = plan.rows, plan.heads
    st = joined(stats[...], stats_got[...], full_width // 2)
    centre = st[0] / full_width
    inv = 1.0 / jnp.sqrt(st[1] / full_width + eps_norm)
    for i, row in enumerate((centre, inv, st[2] / full_width, st[3] * inv / full_width)):
        cols[i] = jnp.transpose(jnp.broadcast_to(row, (HEAD_DIM, 2 * rows)))

    def one(h, slot):
        mine = own_lanes(meta, heads, h)
        scale, shift = gain[:, mine], bias[:, mine]
        res = (so[:, mine], sc_got[1, :, lanes(h)])
        cot = (co[:, mine], sc_got[2, :, lanes(h)])
        for seg in range(2):
            part = slice(seg * rows, (seg + 1) * rows)
            att = attn[h, part, :]
            inv_col = cols[1, part, :]
            normed = (alpha_res * res[seg].astype(f32) + att - cols[0, part, :]) * inv_col
            if seg == 0:
                n_own[:, lanes(h)] = (scale * normed + shift).astype(bf16)
            else:
                n_send[h] = (scale * normed + shift).astype(bf16)
            g = cot[seg].astype(f32) * scale
            da = (inv_col * (g - cols[2, part, :] - normed * cols[3, part, :])).astype(bf16)
            da_out[h, part, :] = da
            da_f = da.astype(f32)
            da_wide[slot, part, :] = da_f
            delta = jnp.broadcast_to(jnp.sum(da_f * att, axis=1, keepdims=True), (rows, HEAD_DIM))
            delta_wide[slot, part, :] = delta
            delta_out[h, part, :] = delta
        for branch, msg, q_rows in zip(FAR, (m2, m3, m4), q_far):
            taken = plan.taken(branch)
            where = [member_rows(meta, off, heads, branch, h, taken, seg * rows) for seg in range(2)]
            picked = jnp.concatenate([da_wide[slot, w, :] for w in where], axis=0)
            msg[0, 0, h, : 2 * taken, :] = picked.astype(bf16)
            pad = [jnp.zeros((HEAD_DIM - 2 * taken, HEAD_DIM), f32)] if 2 * taken < HEAD_DIM else []
            lse_rows = jnp.concatenate([lse[h, w, :] for w in where] + pad, axis=0)
            delta_rows = jnp.concatenate([delta_wide[slot, w, :] for w in where] + pad, axis=0)
            msg[0, 0, h, 2 * taken + STAT_ROWS :, :] = q_rows[0, 0, h]
            msg[0, 0, h, 2 * taken : 2 * taken + STAT_ROWS, :] = split_rows(
                jnp.transpose(lse_rows)[0:1], jnp.transpose(delta_rows)[0:1]
            )

    plan.each_head(together, one)


def norm(plan, full_width, stats, stats_got, attn, lse, stream, cot, sc_got, gain, bias, q_far):
    rows, heads = plan.rows, plan.heads
    sd = jax.ShapeDtypeStruct
    together = 2
    outs = [
        sd((rows, plan.width), bf16),
        sd((heads, rows, HEAD_DIM), bf16),
        sd((heads, 2 * rows, HEAD_DIM), bf16),
        sd((heads, 2 * rows, HEAD_DIM), f32),
    ] + [sd((1, 1, heads, 4 * plan.taken(b) + STAT_ROWS, HEAD_DIM), bf16) for b in FAR]
    wide_rows = pltpu.VMEM((together, 2 * rows, HEAD_DIM), f32)
    return plan.call(
        functools.partial(norm_body, plan, full_width, together),
        [stats, stats_got, attn, lse, stream, cot, sc_got, gain, bias, *q_far],
        outs,
        [pltpu.VMEM((4, 2 * rows, HEAD_DIM), f32), wide_rows, wide_rows],
        name="norm",
    )


def dscores(query, key, value, grad, lse, delta):
    reach = key.shape[0] // HEAD_DIM
    probs = jnp.exp2(dot_nt(query, key) * scaling2 - wide(lse, reach))
    dprob = dot_nt(grad, value)
    return probs.astype(bf16), (probs * (dprob - wide(delta, reach))).astype(bf16)


def near_backward_body(plan, layouts, first_head, count, meta, off, *refs):
    counts = [len(x) for x in layouts]
    qo, ko, vo, kv_got, q_got, da, lse, delta = refs[:8]
    pieces = refs[8 : 8 + sum(counts)]
    own, *sends, wide_in, sums = refs[-6:]
    rows, heads = plan.rows, plan.heads

    def one(i, slot):
        h = first_head + i
        mine = own_lanes(meta, heads, h)
        seg_in = (
            (qo[:, mine], ko[:, mine], vo[:, mine], da[h, :rows, :]),
            (q_got[0, :, lanes(h)], kv_got[0, :, lanes(h)], kv_got[1, :, lanes(h)], da[h, rows:, :]),
        )
        for seg in range(2):
            for t in range(4):
                wide_in[slot, 2 * t + seg] = seg_in[seg][t].astype(f32)
        for seg in range(2):
            part = slice(seg * rows, (seg + 1) * rows)
            q, k, v, grad = seg_in[seg]
            probs, ds = dscores(q, k, v, grad, lse[h, part, :], delta[h, part, :])
            sums[slot, 0, part, :] = dot_nn(ds, k)
            sums[slot, 1, part, :] = dot_tn(ds, q)
            sums[slot, 2, part, :] = dot_tn(probs, grad)
        for branch in range(1, BRANCHES + 1):
            taken = plan.taken(branch)
            inside = member_rows(meta, off, heads, branch, h, taken)
            where = [member_rows(meta, off, heads, branch, h, taken, seg * rows) for seg in range(2)]

            def member(t):
                picked = [wide_in[slot, 2 * t + seg, inside, :] for seg in range(2)]
                return jnp.concatenate(picked, axis=0).astype(bf16)

            query, grad = member(0), member(3)
            lse_rows = jnp.concatenate([lse[h, w, :] for w in where], axis=0)
            delta_rows = jnp.concatenate([delta[h, w, :] for w in where], axis=0)
            if branch == 1:
                key, value = member(1), member(2)
            else:
                first = sum(counts[: branch - 2])
                far = pieces[first : first + counts[branch - 2]]
                layout = layouts[branch - 2]
                key, value = gathered(far, layout, 0, h), gathered(far, layout, 1, h)
            probs, ds = dscores(query, key, value, grad, lse_rows, delta_rows)
            grads = [dot_nn(ds, key)]
            if branch == 1:
                grads += [dot_tn(ds, query), dot_tn(probs, grad)]
            for t, rows_new in enumerate(grads):
                for seg in range(2):
                    sums[slot, t, where[seg], :] = (
                        sums[slot, t, where[seg], :] + rows_new[seg * taken : (seg + 1) * taken]
                    )
        for t, scale in enumerate((scaling, scaling, None)):
            both = sums[slot, t]
            both = both if scale is None else both * scale
            own[t, h] = both[:rows]
            sends[t][h] = both[rows:].astype(bf16)

    together = min(2, count)

    def step(i, carry):
        for slot in range(together):
            one(i * together + slot, slot)
        return carry

    lax.fori_loop(0, count // together, step, 0)


def near_backward(plan, first_head, count, ins, pieces, before=(), wait_for=()):
    shape = (plan.heads, plan.rows, HEAD_DIM)
    flat = [*ins, *[x.array for p in pieces for x in p]]
    return plan.call(
        functools.partial(near_backward_body, plan, [extents(p) for p in pieces], first_head, count),
        [*flat, *before],
        [jax.ShapeDtypeStruct((3, *shape), f32)] + [jax.ShapeDtypeStruct(shape, bf16)] * 3,
        [pltpu.VMEM((2, 8, plan.rows, HEAD_DIM), f32), pltpu.VMEM((2, 3, 2 * plan.rows, HEAD_DIM), f32)],
        name=f"near_backward{first_head}",
        aliases={len(flat) + 2 + i: i for i in range(len(before))},
        wait_for=wait_for,
    )


def far_backward_body(plan, branches, layouts, meta, off, *refs):
    counts = [len(x) for x in layouts]
    kvs, msgs, (own, send) = refs[: len(branches)], refs[len(branches) : -2], refs[-2:]

    def one(h, slot):
        row = 0
        for j, branch in enumerate(branches):
            taken = plan.taken(branch)
            grads, queries, halves_of = [], [], [None] * (plan.rows // HEAD_DIM)
            place = 0
            mine = msgs[sum(counts[:j]) : sum(counts[: j + 1])]
            for ref, (many, start, _) in zip(mine, layouts[j], strict=True):
                table_at = start + 2 * taken
                for n in range(many):
                    grads.append(ref[n, 0, h, start:table_at, :])
                    queries.append(ref[n, 0, h, table_at + STAT_ROWS : table_at + STAT_ROWS + 2 * taken, :])
                    terms = ref[n, 0, h, table_at : table_at + STAT_ROWS, :].astype(f32)
                    half, shift = divmod(place, HEAD_DIM)
                    if shift:
                        terms = pltpu.roll(terms, shift, 1)
                    halves_of[half] = terms if halves_of[half] is None else halves_of[half] + terms
                    place += 2 * taken
            grad = jnp.concatenate(grads, axis=0)
            query = jnp.concatenate(queries, axis=0)
            table = jnp.concatenate(halves_of, axis=1)
            lse = table[0:1] + table[1:2] + table[2:3]
            delta = table[3:4] + table[4:5]
            key, value = kvs[j][0, 0, h], kvs[j][0, 1, h]
            probs = jnp.exp2(dot_nt(key, query) * scaling2 - lse)
            ds = (probs * (dot_nt(value, grad) - delta)).astype(bf16)
            dkey = dot_nn(ds, query) * scaling
            dvalue = dot_nn(probs.astype(bf16), grad)
            for i, rows in enumerate((dkey, dvalue)):
                own[i, h, row : row + taken, :] = rows[:taken]
                send[i, h, row : row + taken, :] = rows[taken:].astype(bf16)
            row += taken

    plan.each_head(4, one)


def far_backward(plan, branches, kvs, pieces, wait_for=()):
    shape = (2, plan.heads, sum(plan.taken(b) for b in branches), HEAD_DIM)
    return plan.call(
        functools.partial(far_backward_body, plan, branches, [extents(p) for p in pieces]),
        [*kvs, *[x.array for p in pieces for x in p]],
        [jax.ShapeDtypeStruct(shape, f32), jax.ShapeDtypeStruct(shape, bf16)],
        name=f"far_backward{branches[0]}",
        wait_for=wait_for,
    )


def column_of(plan, meta, slot):
    heads = plan.heads
    core = meta[0] if slot < heads else 1 - meta[0]
    return core * heads + slot % heads


def column_lanes(plan, meta, slot):
    return pl.ds(pl.multiple_of(column_of(plan, meta, slot) * HEAD_DIM, HEAD_DIM), HEAD_DIM)


def finish_q_body(plan, meta, off, own, got, n_own, n_got, dq, normed, mark, wide_got, sems):
    copies = []

    def send(src, dst):
        copy = pltpu.make_async_copy(src, dst, sems.at[len(copies)])
        copy.start()
        copies.append(copy)

    mine = pl.ds(pl.multiple_of(meta[0] * plan.width, plan.width), plan.width)
    send(n_own, normed.at[:, mine])
    for i in range(plan.heads):
        theirs = column_lanes(plan, meta, plan.heads + i)
        send(own.at[0, i], dq.at[:, column_lanes(plan, meta, i)])
        send(n_got.at[i], normed.at[:, theirs])
        wide_got[i] = got[i].astype(f32)
        send(wide_got.at[i], dq.at[:, theirs])
    for copy in copies:
        copy.wait()
    mark[...] = jnp.zeros_like(mark)


def finish_q(plan, own, got, n_own, n_got):
    full = (plan.rows, 2 * plan.width)
    return plan.call(
        functools.partial(finish_q_body, plan),
        [own, got, n_own, n_got],
        [
            jax.ShapeDtypeStruct(full, f32),
            jax.ShapeDtypeStruct(full, bf16),
            jax.ShapeDtypeStruct((8, HEAD_DIM), f32),
        ],
        [
            pltpu.VMEM((plan.heads, plan.rows, HEAD_DIM), f32),
            pltpu.SemaphoreType.DMA((3 * plan.heads + 1,)),
        ],
        name="finish_q",
        out_place=[pltpu.HBM, pltpu.HBM, pltpu.VMEM],
    )


def fold_body(plan, branches, meta, off, *refs):
    own, got, row_refs, sums = refs[0], refs[1:3], refs[3:5], refs[5]
    for slot in range(2 * plan.heads):
        side, h = divmod(slot, plan.heads)
        for t in range(2):
            sums[t, slot] = own[1 + t, h] if side == 0 else got[t][h].astype(f32)
        row = 0
        for branch in branches:
            taken = plan.taken(branch)
            start = off[branch - 1, meta[1] + column_of(plan, meta, slot)]
            where = pl.ds(start, taken, stride=2**branch)
            for t in range(2):
                rows = row_refs[side][t, h, row : row + taken, :].astype(f32)
                sums[t, slot, where, :] = sums[t, slot, where, :] + rows
            row += taken


def fold(plan, branches, own, got, rows_own, rows_got):
    shape = (2, 2 * plan.heads, plan.rows, HEAD_DIM)
    return plan.call(
        functools.partial(fold_body, plan, branches),
        [own, *got, rows_own, rows_got],
        [jax.ShapeDtypeStruct(shape, f32)],
        name="fold",
    )[0]


def finish_kv_body(plan, branch, meta, off, given, own, got, dk, dv, sums, sems):
    copies = []
    for slot in range(2 * plan.heads):
        taken = plan.taken(branch)
        start = off[branch - 1, meta[1] + column_of(plan, meta, slot)]
        where = pl.ds(start, taken, stride=2**branch)
        rows = (own, got)[slot // plan.heads]
        for t, out in enumerate((dk, dv)):
            sums[t, slot] = given[t, slot]
            sums[t, slot, where, :] = given[t, slot, where, :] + rows[t, slot % plan.heads].astype(f32)
            copy = pltpu.make_async_copy(
                sums.at[t, slot], out.at[:, column_lanes(plan, meta, slot)], sems.at[len(copies)]
            )
            copy.start()
            copies.append(copy)
    for copy in copies:
        copy.wait()


def finish_kv(plan, branch, sums, own, got):
    full = jax.ShapeDtypeStruct((plan.rows, 2 * plan.width), f32)
    return plan.call(
        functools.partial(finish_kv_body, plan, branch),
        [sums, own, got],
        [full, full],
        [pltpu.VMEM(sums.shape, f32), pltpu.SemaphoreType.DMA((4 * plan.heads,))],
        name="finish_kv",
        out_place=pltpu.HBM,
    )


def gather(plan, msgs, filler, last_filler=None):
    two, three, four = msgs
    four_far, three_y, three_z = flip(four, "seq", 8), flip(three, "seq", 2), flip(three, "seq", 4)
    two_y = flip(two, "seq", 2)
    both, for_z = relay(plan, three_y, four, four_far, [filler(), three_z])
    four_y, from_z = flip(both, "seq", 2), flip(for_z, "seq", 4)
    four_yz = flip(last_filler(four_y, both) if last_filler else four_y, "seq", 4)
    rows_three, rows_four = three.shape[3], four.shape[3]
    from_z_four = [Rows(from_z, rows_three + i * rows_four, rows_four) for i in range(2)]
    return (
        [whole_rows(x) for x in (two, two_y)],
        [whole_rows(x) for x in (three, three_y, three_z)] + [Rows(from_z, 0, rows_three)],
        [whole_rows(x) for x in (four, four_far, four_y)] + from_z_four + [whole_rows(four_yz)],
    )


def shards(queries, key_rows, value_rows, stream, norm_gain, norm_bias, head_offsets, cotangent):
    rows = queries.shape[0]
    heads_here = queries.shape[1] // HEAD_DIM
    half = queries.shape[1] // 2
    core = lax.axis_index("seq") & 1
    first_head = lax.axis_index("head") * heads_here
    meta = jnp.stack([core, first_head]).astype(jnp.int32)
    plan = Plan(rows, heads_here, meta, head_offsets)
    gain, bias = norm_gain[None, :], norm_bias[None, :]

    kv_got = flip(halves(plan, [key_rows, value_rows]), "seq", 1)
    qsc_got = flip(halves(plan, [queries, stream, cotangent]), "seq", 1)
    kv_far = pick(plan, [key_rows, value_rows], kv_got, 0)
    near = near_forward(plan, queries, key_rows, value_rows, kv_got, qsc_got)
    kv_pieces = gather(plan, kv_far, lambda: near[1])
    q_far = pick(plan, [queries], qsc_got, 0)
    far = [far_forward(plan, b, q_far[b - 2], kv_pieces[b - 2]) for b in FAR]
    attn, lse, stats = combine(plan, near, far, stream, cotangent, qsc_got, gain)

    stats = join(plan, stats, flip(stats, "seq", 1), half, swap=True)
    width, mask = 4 * half, 1
    while 2 * mask < lax.axis_size("head"):
        stats = join(plan, stats, flip(stats, "head", mask), width // 2)
        width, mask = 2 * width, 2 * mask
    n_own, n_send, da, delta, *msgs = norm(
        plan,
        width,
        stats,
        flip(stats, "head", mask),
        attn,
        lse,
        stream,
        cotangent,
        qsc_got,
        gain,
        bias,
        q_far,
    )

    n_got = flip(n_send, "seq", 1)
    ins = [queries, key_rows, value_rows, kv_got, qsc_got, da, lse, delta]
    first = max(1, plan.heads // 4)
    parts = []

    def near_first():
        parts.append(near_backward(plan, 0, first, ins, kv_pieces))
        return parts[-1][0]

    def near_rest(four_y, both):
        own, *sends = near_backward(
            plan, first, plan.heads - first, ins, kv_pieces, parts[-1], wait_for=[both, n_got]
        )
        four_y, own = lax.optimization_barrier((four_y, own))
        parts.append((own, *sends))
        return four_y

    msg_pieces = gather(plan, msgs, near_first, near_rest)
    own, *sends = parts[-1]
    got_q, *got_kv = [flip(send, "seq", 1) for send in sends]
    grad_query, normed_out, mark = finish_q(plan, own, got_q, n_own, n_got)
    rows_own, rows_send = far_backward(plan, FAR[:-1], kv_far[:-1], msg_pieces[:-1], [own])
    sums = fold(plan, FAR[:-1], own, got_kv, rows_own, flip(rows_send, "seq", 1))
    rows_own, rows_send = far_backward(plan, FAR[-1:], kv_far[-1:], msg_pieces[-1:], [mark, sums])
    grad_key, grad_value = finish_kv(plan, FAR[-1], sums, rows_own, flip(rows_send, "seq", 1))
    return normed_out, grad_query, grad_key, grad_value


def solution(mesh):
    return jax.shard_map(
        shards,
        mesh=mesh,
        in_specs=(
            P("seq", "head"),
            P("seq", "head"),
            P("seq", "head"),
            P("seq", "head"),
            P("head"),
            P("head"),
            P(),
            P("seq", "head"),
        ),
        out_specs=(P("seq", "head"), P("seq", "head"), P("seq", "head"), P("seq", "head")),
        check_vma=False,
    )
```

```python
import functools
import math
from typing import NamedTuple

import jax
import jax.numpy as jnp
from jax import lax
from jax.experimental import pallas as pl
from jax.experimental.pallas import tpu as pltpu
from jax.sharding import PartitionSpec as P

HEAD_DIM = 128
BRANCHES = 4
FAR = (2, 3, 4)
GROUPS = ((2, 3), (4,))
STAT_ROWS = 8
COPIES = 4

alpha_res = (2.0 * 24.0) ** 0.25
eps_norm = 1e-05
scaling = HEAD_DIM ** (-0.5)
scaling2 = scaling * math.log2(math.e)

f32 = jnp.float32
bf16 = jnp.bfloat16


def dot_nt(a, b):
    return lax.dot_general(a, b, (((1,), (1,)), ((), ())), preferred_element_type=f32)


def dot_nn(a, b):
    return lax.dot_general(a, b, (((1,), (0,)), ((), ())), preferred_element_type=f32)


def dot_tn(a, b):
    return lax.dot_general(a, b, (((0,), (0,)), ((), ())), preferred_element_type=f32)


def flip(block, axis, mask):
    count = lax.axis_size(axis)
    return lax.ppermute(block, axis, [(i, i ^ mask) for i in range(count)])


def wide(column_block, times):
    return jnp.concatenate([column_block] * times, axis=1)


def attend(query, key, value):
    scores = dot_nt(query, key)
    peak = jnp.max(scores, axis=1, keepdims=True)
    weights = jnp.exp2((scores - peak) * scaling2).astype(bf16)
    both = dot_nn(weights, jnp.concatenate([value, jnp.ones_like(value)], axis=1))
    total = both[:, HEAD_DIM:]
    return both[:, :HEAD_DIM] / total, peak * scaling2 + jnp.log2(total)


def merged(out_a, lse_a, out_b, lse_b):
    peak = jnp.maximum(lse_a, lse_b)
    part_a = jnp.exp2(lse_a - peak)
    part_b = jnp.exp2(lse_b - peak)
    total = part_a + part_b
    return (out_a * part_a + out_b * part_b) / total, peak + jnp.log2(total)


def room(scratch):
    arrays = [x for x in scratch if not isinstance(x, pltpu.SemaphoreType) and hasattr(x, "memory_space")]
    arrays = [x for x in arrays if x.memory_space == pltpu.VMEM]
    return sum(math.prod(x.shape) * jnp.dtype(x.dtype).itemsize for x in arrays) + 4 * 2**20


class Plan:
    def __init__(self, rows, heads_here, meta, offsets):
        self.rows = rows
        self.heads = heads_here // 2
        self.width = self.heads * HEAD_DIM
        self.meta = meta
        self.offsets = offsets

    def taken(self, branch):
        return self.rows >> branch

    def call(
        self,
        body,
        ins,
        outs,
        scratch=(),
        name=None,
        in_place=pltpu.VMEM,
        out_place=pltpu.VMEM,
        aliases=None,
        wait_for=(),
    ):
        given, waited = 2 + len(ins), len(wait_for)

        def without_waited(*refs):
            body(*refs[:given], *refs[given + waited :])

        scalars = pl.BlockSpec(memory_space=pltpu.SMEM)
        return pl.pallas_call(
            without_waited if waited else body,
            out_shape=outs,
            in_specs=[scalars, scalars]
            + [pl.BlockSpec(memory_space=in_place)] * len(ins)
            + [pl.BlockSpec(memory_space=pl.ANY)] * waited,
            out_specs=[
                pl.BlockSpec(memory_space=out_place[i] if isinstance(out_place, list) else out_place)
                for i in range(len(outs))
            ],
            scratch_shapes=list(scratch),
            compiler_params=pltpu.CompilerParams(vmem_limit_bytes=room(scratch)),
            cost_estimate=pl.CostEstimate(flops=0, bytes_accessed=0, transcendentals=0),
            input_output_aliases=aliases or {},
            name=name,
        )(self.meta, self.offsets, *ins, *wait_for)

    def each_head(self, together, body):
        together = min(together, self.heads)
        if together == self.heads:
            for h in range(self.heads):
                body(h, h)
            return

        def step(i, carry):
            for slot in range(together):
                body(i * together + slot, slot)
            return carry

        lax.fori_loop(0, self.heads // together, step, 0)


def lanes(h):
    if isinstance(h, int):
        return slice(h * HEAD_DIM, (h + 1) * HEAD_DIM)
    return pl.ds(pl.multiple_of(h * HEAD_DIM, HEAD_DIM), HEAD_DIM)


def own_lanes(meta, heads, h):
    return pl.ds(pl.multiple_of((meta[0] * heads + h) * HEAD_DIM, HEAD_DIM), HEAD_DIM)


def member_rows(meta, off, heads, branch, h, taken, shift=0):
    start = off[branch - 1, meta[1] + meta[0] * heads + h]
    return pl.ds(start + shift, taken, stride=2**branch)


def halves_body(plan, count, meta, off, *refs):
    ins, out, sems = refs[:count], refs[count], refs[count + 1]
    other = pl.ds(pl.multiple_of((1 - meta[0]) * plan.width, plan.width), plan.width)
    step = plan.rows // COPIES
    copies = []
    for i, ref in enumerate(ins):
        for j in range(COPIES):
            rows = slice(j * step, (j + 1) * step)
            sem = sems.at[i * COPIES + j]
            copies.append(pltpu.make_async_copy(ref.at[rows, other], out.at[i, rows], sem))
    for copy in copies:
        copy.start()
    for copy in copies:
        copy.wait()


def halves(plan, blocks, wait_for=()):
    count = len(blocks)
    out = jax.ShapeDtypeStruct((count, plan.rows, plan.width), blocks[0].dtype)
    return plan.call(
        functools.partial(halves_body, plan, count),
        [pltpu.with_memory_space_constraint(x, pltpu.HBM) for x in blocks],
        [out],
        [pltpu.SemaphoreType.DMA((count * COPIES,))],
        name="halves",
        wait_for=wait_for,
        in_place=pltpu.HBM,
    )[0]


def pick_body(plan, count, first, meta, off, *refs):
    owns, got, outs, scratch = refs[:count], refs[count], refs[count + 1 : count + 4], refs[-1]
    heads, rows = plan.heads, plan.rows

    def one(h, slot):
        for i in range(count):
            scratch[slot, 2 * i] = owns[i][:, own_lanes(meta, heads, h)].astype(f32)
            scratch[slot, 2 * i + 1] = got[first + i, :, lanes(h)].astype(f32)
        for branch, out in zip(FAR, outs):
            taken = plan.taken(branch)
            where = member_rows(meta, off, heads, branch, h, taken)
            for i in range(count):
                picked = [scratch[slot, 2 * i + seg, where, :] for seg in range(2)]
                out[0, i, h] = jnp.concatenate(picked, axis=0).astype(bf16)

    plan.each_head(4, one)


def pick(plan, owns, got, first):
    count = len(owns)
    outs = [
        jax.ShapeDtypeStruct((1, count, plan.heads, 2 * plan.taken(b), HEAD_DIM), bf16) for b in FAR
    ]
    return plan.call(
        functools.partial(pick_body, plan, count, first),
        [*owns, got],
        outs,
        [pltpu.VMEM((4, 2 * count, plan.rows, HEAD_DIM), f32)],
        name="pick",
    )


def near_forward_body(plan, together, meta, off, qo, ko, vo, kv_got, q_got, out, lse, wide_in, acc, acc_l):
    heads, rows, taken = plan.heads, plan.rows, plan.taken(1)

    def one(h, slot):
        mine = own_lanes(meta, heads, h)
        seg_in = (
            (qo[:, mine], ko[:, mine], vo[:, mine]),
            (q_got[0, :, lanes(h)], kv_got[0, :, lanes(h)], kv_got[1, :, lanes(h)]),
        )
        for seg in range(2):
            for i in range(3):
                wide_in[slot, 2 * i + seg] = seg_in[seg][i].astype(f32)
        where = member_rows(meta, off, heads, 1, h, taken)
        near = []
        for i in range(3):
            picked = [wide_in[slot, 2 * i + seg, where, :] for seg in range(2)]
            near.append(jnp.concatenate(picked, axis=0).astype(bf16))
        for seg in range(2):
            o, l2 = attend(*seg_in[seg])
            acc[slot, seg] = o
            acc_l[slot, seg] = l2
        o, l2 = attend(*near)
        for seg in range(2):
            part = slice(seg * taken, (seg + 1) * taken)
            new_o, new_l = merged(
                acc[slot, seg, where, :], acc_l[slot, seg, where, :], o[part], l2[part]
            )
            acc[slot, seg, where, :] = new_o
            acc_l[slot, seg, where, :] = new_l
        for seg in range(2):
            part = slice(seg * rows, (seg + 1) * rows)
            out[h, part, :] = acc[slot, seg]
            lse[h, part, :] = acc_l[slot, seg]

    plan.each_head(together, one)


def near_forward(plan, q, k, v, kv_got, q_got):
    rows, heads = plan.rows, plan.heads
    together = 2
    out = jax.ShapeDtypeStruct((heads, 2 * rows, HEAD_DIM), f32)
    pair = pltpu.VMEM((together, 2, rows, HEAD_DIM), f32)
    return plan.call(
        functools.partial(near_forward_body, plan, together),
        [q, k, v, kv_got, q_got],
        [out, out],
        [pltpu.VMEM((together, 6, rows, HEAD_DIM), f32), pair, pair],
        name="near_forward",
    )


class Rows(NamedTuple):
    array: jax.Array
    start: int
    count: int


def whole_rows(array):
    return Rows(array, 0, array.shape[3])


def extents(pieces):
    return [(p.array.shape[0], p.start, p.count) for p in pieces]


def gathered(refs, layout, which, h):
    parts = []
    for ref, (many, start, count) in zip(refs, layout, strict=True):
        for n in range(many):
            parts.append(ref[n, which, h, start : start + count, :])
    return jnp.concatenate(parts, axis=0)


def far_forward_body(plan, layout, meta, off, q, *refs):
    pieces, out, lse = refs[:-2], refs[-2], refs[-1]

    def one(h, slot):
        o, l2 = attend(q[0, 0, h], gathered(pieces, layout, 0, h), gathered(pieces, layout, 1, h))
        out[h] = o
        lse[h] = l2

    plan.each_head(4, one)


def far_forward(plan, branch, q, pieces):
    rows, heads = 2 * plan.taken(branch), plan.heads
    outs = [jax.ShapeDtypeStruct((heads, rows, HEAD_DIM), f32)] * 2
    return plan.call(
        functools.partial(far_forward_body, plan, extents(pieces)),
        [q, *[p.array for p in pieces]],
        outs,
        name=f"far_forward{branch}",
    )


def combine_body(plan, meta, off, *refs):
    near_o, near_l, far, (so, co, sc_got, gain) = refs[0], refs[1], refs[2:8], refs[8:12]
    attn, lse, stats, pre_all, g_all = refs[12:]
    rows, heads = plan.rows, plan.heads

    def one(h, slot):
        mine = own_lanes(meta, heads, h)
        attn[h] = near_o[h]
        lse[h] = near_l[h]
        for i, branch in enumerate(FAR):
            taken = plan.taken(branch)
            for seg in range(2):
                where = member_rows(meta, off, heads, branch, h, taken, seg * rows)
                part = slice(seg * taken, (seg + 1) * taken)
                new_o, new_l = merged(
                    attn[h, where, :], lse[h, where, :], far[2 * i][h, part], far[2 * i + 1][h, part]
                )
                attn[h, where, :] = new_o
                lse[h, where, :] = new_l
        scale = gain[:, mine]
        res = (so[:, mine], sc_got[1, :, lanes(h)])
        cot = (co[:, mine], sc_got[2, :, lanes(h)])
        for seg in range(2):
            part = slice(seg * rows, (seg + 1) * rows)
            pre_all[h, part, :] = alpha_res * res[seg].astype(f32) + attn[h, part, :]
            g_all[h, part, :] = cot[seg].astype(f32) * scale

    plan.each_head(2, one)

    def total(i, acc):
        return acc + pre_all[i]

    for seg in range(2):
        part = slice(seg * rows, (seg + 1) * rows)
        acc = pre_all[0, part, :]
        for i in range(1, heads):
            acc = acc + pre_all[i, part, :]
        pre_sum = jnp.sum(acc, axis=1, keepdims=True)
        centre = pre_sum / (heads * HEAD_DIM)
        second = jnp.zeros((rows, HEAD_DIM), f32)
        g_sum, cross = second, second
        for i in range(heads):
            diff = pre_all[i, part, :] - centre
            g = g_all[i, part, :]
            second, g_sum, cross = second + diff * diff, g_sum + g, cross + g * diff
        lane = lax.broadcasted_iota(jnp.int32, (rows, HEAD_DIM), 1)
        table = jnp.broadcast_to(pre_sum, (rows, HEAD_DIM))
        for i, x in enumerate((second, g_sum, cross)):
            table = jnp.where(lane == i + 1, jnp.sum(x, axis=1, keepdims=True), table)
        stats[:, part] = jnp.transpose(table)[:STAT_ROWS]


def combine(plan, near, far, stream, cot, sc_got, gain):
    rows, heads = plan.rows, plan.heads
    per_head = jax.ShapeDtypeStruct((heads, 2 * rows, HEAD_DIM), f32)
    outs = [per_head, per_head, jax.ShapeDtypeStruct((STAT_ROWS, 2 * rows), f32)]
    return plan.call(
        functools.partial(combine_body, plan),
        [*near, *[x for pair in far for x in pair], stream, cot, sc_got, gain],
        outs,
        [pltpu.VMEM((heads, 2 * rows, HEAD_DIM), f32)] * 2,
        name="combine",
    )


def joined(mine, other, count):
    gap = (mine[0:1] - other[0:1]) / count
    return [
        mine[0:1] + other[0:1],
        mine[1:2] + other[1:2] + gap * gap * (count / 2),
        mine[2:3] + other[2:3],
        mine[3:4] + other[3:4] + gap * 0.5 * (mine[2:3] - other[2:3]),
    ]


def join_body(rows, count, swap, meta, off, mine, other, out):
    theirs = other[...]
    if swap:
        theirs = jnp.concatenate([theirs[:, rows:], theirs[:, :rows]], axis=1)
    for i, row in enumerate(joined(mine[...], theirs, count)):
        out[i : i + 1, :] = row


def join(plan, mine, other, count, swap=False):
    return plan.call(
        functools.partial(join_body, plan.rows, count, swap),
        [mine, other],
        [jax.ShapeDtypeStruct(mine.shape, f32)],
        name="join",
    )[0]


def relay_body(meta, off, three, four, four_far, both, for_z):
    both[0:1] = four[...]
    both[1:2] = four_far[...]
    place = 0
    for ref in (three, four, four_far):
        rows = ref.shape[3]
        for c in range(ref.shape[1]):
            for h in range(ref.shape[2]):
                for_z[0, c, h, place : place + rows, :] = ref[0, c, h]
        place += rows


def relay(plan, three, four, four_far, wait_for):
    _, tensors, heads, rows, width = four.shape
    sd = jax.ShapeDtypeStruct
    outs = [
        sd((2, tensors, heads, rows, width), four.dtype),
        sd((1, tensors, heads, three.shape[3] + 2 * rows, width), four.dtype),
    ]
    return plan.call(relay_body, [three, four, four_far], outs, name="relay", wait_for=wait_for)


def split_rows(lse, delta):
    high = lse.astype(bf16).astype(f32)
    mid = (lse - high).astype(bf16).astype(f32)
    low = lse - high - mid
    delta_high = delta.astype(bf16).astype(f32)
    delta_low = delta - delta_high
    return jnp.concatenate(
        [high, mid, low, delta_high, delta_low] + [jnp.zeros_like(lse)] * (STAT_ROWS - 5), axis=0
    ).astype(bf16)


def norm_body(plan, full_width, together, meta, off, *refs):
    stats, stats_got, attn, lse, so, co, sc_got, gain, bias = refs[:9]
    q_far = (None, *refs[9:11])
    n_own, n_send, da_out, delta_out, m2, m3, m4, cols, da_wide, delta_wide = refs[11:]
    rows, heads = plan.rows, plan.heads
    st = joined(stats[...], stats_got[...], full_width // 2)
    centre = st[0] / full_width
    inv = 1.0 / jnp.sqrt(st[1] / full_width + eps_norm)
    for i, row in enumerate((centre, inv, st[2] / full_width, st[3] * inv / full_width)):
        cols[i] = jnp.transpose(jnp.broadcast_to(row, (HEAD_DIM, 2 * rows)))

    def one(h, slot):
        mine = own_lanes(meta, heads, h)
        scale, shift = gain[:, mine], bias[:, mine]
        res = (so[:, mine], sc_got[1, :, lanes(h)])
        cot = (co[:, mine], sc_got[2, :, lanes(h)])
        for seg in range(2):
            part = slice(seg * rows, (seg + 1) * rows)
            att = attn[h, part, :]
            inv_col = cols[1, part, :]
            normed = (alpha_res * res[seg].astype(f32) + att - cols[0, part, :]) * inv_col
            if seg == 0:
                n_own[:, lanes(h)] = (scale * normed + shift).astype(bf16)
            else:
                n_send[h] = (scale * normed + shift).astype(bf16)
            g = cot[seg].astype(f32) * scale
            da = (inv_col * (g - cols[2, part, :] - normed * cols[3, part, :])).astype(bf16)
            da_out[h, part, :] = da
            da_f = da.astype(f32)
            da_wide[slot, part, :] = da_f
            delta = jnp.broadcast_to(jnp.sum(da_f * att, axis=1, keepdims=True), (rows, HEAD_DIM))
            delta_wide[slot, part, :] = delta
            delta_out[h, part, :] = delta
        for branch, msg, q_rows in zip(FAR, (m2, m3, m4), q_far):
            taken = plan.taken(branch)
            where = [member_rows(meta, off, heads, branch, h, taken, seg * rows) for seg in range(2)]
            picked = jnp.concatenate([da_wide[slot, w, :] for w in where], axis=0)
            msg[0, 0, h, : 2 * taken, :] = picked.astype(bf16)
            pad = [jnp.zeros((HEAD_DIM - 2 * taken, HEAD_DIM), f32)] if 2 * taken < HEAD_DIM else []
            lse_rows = jnp.concatenate([lse[h, w, :] for w in where] + pad, axis=0)
            delta_rows = jnp.concatenate([delta_wide[slot, w, :] for w in where] + pad, axis=0)
            if q_rows is not None:
                msg[0, 0, h, 2 * taken + STAT_ROWS :, :] = q_rows[0, 0, h]
            msg[0, 0, h, 2 * taken : 2 * taken + STAT_ROWS, :] = split_rows(
                jnp.transpose(lse_rows)[0:1], jnp.transpose(delta_rows)[0:1]
            )

    plan.each_head(together, one)


def norm(plan, full_width, stats, stats_got, attn, lse, stream, cot, sc_got, gain, bias, q_far, wait_for):
    rows, heads = plan.rows, plan.heads
    sd = jax.ShapeDtypeStruct
    together = 2
    outs = [
        sd((rows, plan.width), bf16),
        sd((heads, rows, HEAD_DIM), bf16),
        sd((heads, 2 * rows, HEAD_DIM), bf16),
        sd((heads, 2 * rows, HEAD_DIM), f32),
    ] + [sd((1, 1, heads, (2 if b == 2 else 4) * plan.taken(b) + STAT_ROWS, HEAD_DIM), bf16) for b in FAR]
    wide_rows = pltpu.VMEM((together, 2 * rows, HEAD_DIM), f32)
    return plan.call(
        functools.partial(norm_body, plan, full_width, together),
        [stats, stats_got, attn, lse, stream, cot, sc_got, gain, bias, *q_far],
        outs,
        [pltpu.VMEM((4, 2 * rows, HEAD_DIM), f32), wide_rows, wide_rows],
        name="norm",
        wait_for=wait_for,
    )


def probs_and_ds(scores, dprob, lse, delta):
    reach = scores.shape[1] // HEAD_DIM
    probs = jnp.exp2(scores * scaling2 - wide(lse, reach))
    return probs.astype(bf16), (probs * (dprob - wide(delta, reach))).astype(bf16)


def near_backward_body(plan, layouts, first_head, count, meta, off, *refs):
    counts = [len(x) for x in layouts]
    qo, ko, vo, kv_got, q_got, da, lse, delta = refs[:8]
    pieces = refs[8 : 8 + sum(counts)]
    own, *sends, wide_in, sums = refs[-6:]
    rows, heads = plan.rows, plan.heads

    def load(h, slot):
        mine = own_lanes(meta, heads, h)
        seg_in = (
            (qo[:, mine], ko[:, mine], vo[:, mine], da[h, :rows, :]),
            (q_got[0, :, lanes(h)], kv_got[0, :, lanes(h)], kv_got[1, :, lanes(h)], da[h, rows:, :]),
        )
        for seg in range(2):
            for t in range(4):
                wide_in[slot, 2 * t + seg] = seg_in[seg][t].astype(f32)
        return seg_in

    def begin(h, slot, seg_in, branch, seg):
        if branch == 0:
            query, key, value, grad = seg_in[seg]
        else:
            inside = member_rows(meta, off, heads, branch, h, plan.taken(branch))

            def member(t):
                picked = [wide_in[slot, 2 * t + s, inside, :] for s in range(2)]
                return jnp.concatenate(picked, axis=0).astype(bf16)

            query, grad = member(0), member(3)
            if branch == 1:
                key, value = member(1), member(2)
            else:
                first, layout = sum(counts[: branch - 2]), layouts[branch - 2]
                far = pieces[first : first + counts[branch - 2]]
                key, value = gathered(far, layout, 0, h), gathered(far, layout, 1, h)
        return (h, slot, branch, seg, query, key, grad, dot_nt(query, key), dot_nt(grad, value))

    def end(h, slot, branch, seg, query, key, grad, scores, dprob):
        taken = plan.taken(branch)
        if branch == 0:
            where = [slice(seg * rows, (seg + 1) * rows)]
        else:
            where = [member_rows(meta, off, heads, branch, h, taken, s * rows) for s in range(2)]
        lse_rows = jnp.concatenate([lse[h, w, :] for w in where], axis=0)
        delta_rows = jnp.concatenate([delta[h, w, :] for w in where], axis=0)
        probs, ds = probs_and_ds(scores, dprob, lse_rows, delta_rows)
        grads = [dot_nn(ds, key)]
        if branch <= 1:
            grads += [dot_tn(ds, query), dot_tn(probs, grad)]
        for t, rows_new in enumerate(grads):
            for s, w in enumerate(where):
                part = rows_new[s * taken : (s + 1) * taken]
                sums[slot, t, w, :] = part if branch == 0 else sums[slot, t, w, :] + part

    def store(h, slot):
        for t, scale in enumerate((scaling, scaling, None)):
            both = sums[slot, t]
            both = both if scale is None else both * scale
            own[t, h] = both[:rows]
            sends[t][h] = both[rows:].astype(bf16)

    together = min(2, count)
    order = [(0, 0), (0, 1)] + [(branch, 0) for branch in range(1, BRANCHES + 1)]

    def step(i, carry):
        hs = [first_head + i * together + slot for slot in range(together)]
        seg_ins = [load(h, slot) for slot, h in enumerate(hs)]
        waiting = []
        for branch, seg in order:
            for slot, h in enumerate(hs):
                waiting.append(begin(h, slot, seg_ins[slot], branch, seg))
                if len(waiting) > 2:
                    end(*waiting.pop(0))
        for item in waiting:
            end(*item)
        for slot, h in enumerate(hs):
            store(h, slot)
        return carry

    lax.fori_loop(0, count // together, step, 0)


def near_backward(plan, first_head, count, ins, pieces, before=(), wait_for=()):
    shape = (plan.heads, plan.rows, HEAD_DIM)
    flat = [*ins, *[x.array for p in pieces for x in p]]
    return plan.call(
        functools.partial(near_backward_body, plan, [extents(p) for p in pieces], first_head, count),
        [*flat, *before],
        [jax.ShapeDtypeStruct((3, *shape), f32)] + [jax.ShapeDtypeStruct(shape, bf16)] * 3,
        [pltpu.VMEM((2, 8, plan.rows, HEAD_DIM), f32), pltpu.VMEM((2, 3, 2 * plan.rows, HEAD_DIM), f32)],
        name=f"near_backward{first_head}",
        aliases={len(flat) + 2 + i: i for i in range(len(before))},
        wait_for=wait_for,
    )


def far_backward_body(plan, branches, layouts, first_row, meta, off, *refs):
    counts = [len(x) for x in layouts]
    kvs, msgs, (own, send) = refs[: len(branches)], refs[len(branches) : -2], refs[-2:]
    msgs, q_two = msgs[: sum(counts)], msgs[sum(counts) : sum(counts) + 2]

    def one(h, slot):
        row = first_row
        for j, branch in enumerate(branches):
            taken = plan.taken(branch)
            grads, queries, halves_of = [], [], [None] * (plan.rows // HEAD_DIM)
            place = 0
            mine = msgs[sum(counts[:j]) : sum(counts[: j + 1])]
            for ref, (many, start, _) in zip(mine, layouts[j], strict=True):
                table_at = start + 2 * taken
                for n in range(many):
                    grads.append(ref[n, 0, h, start:table_at, :])
                    if branch != 2:
                        queries.append(ref[n, 0, h, table_at + STAT_ROWS : table_at + STAT_ROWS + 2 * taken, :])
                    terms = ref[n, 0, h, table_at : table_at + STAT_ROWS, :].astype(f32)
                    half, shift = divmod(place, HEAD_DIM)
                    if shift:
                        terms = pltpu.roll(terms, shift, 1)
                    halves_of[half] = terms if halves_of[half] is None else halves_of[half] + terms
                    place += 2 * taken
            if branch == 2:
                queries = [ref[0, 0, h] for ref in q_two]
            grad = jnp.concatenate(grads, axis=0)
            query = jnp.concatenate(queries, axis=0)
            table = jnp.concatenate(halves_of, axis=1)
            lse = table[0:1] + table[1:2] + table[2:3]
            delta = table[3:4] + table[4:5]
            key, value = kvs[j][0, 0, h], kvs[j][0, 1, h]
            probs = jnp.exp2(dot_nt(key, query) * scaling2 - lse)
            ds = (probs * (dot_nt(value, grad) - delta)).astype(bf16)
            dkey = dot_nn(ds, query) * scaling
            dvalue = dot_nn(probs.astype(bf16), grad)
            for i, rows in enumerate((dkey, dvalue)):
                own[i, h, row : row + taken, :] = rows[:taken]
                send[i, h, row : row + taken, :] = rows[taken:].astype(bf16)
            row += taken

    plan.each_head(4, one)


def far_backward(plan, branches, kvs, pieces, q_two, wait_for, before=()):
    shape = (2, plan.heads, sum(plan.taken(b) for b in FAR), HEAD_DIM)
    first_row = sum(plan.taken(b) for b in FAR if b < branches[0])
    flat = [*kvs, *[x.array for p in pieces for x in p], *q_two]
    return plan.call(
        functools.partial(far_backward_body, plan, branches, [extents(p) for p in pieces], first_row),
        [*flat, *before],
        [jax.ShapeDtypeStruct(shape, f32), jax.ShapeDtypeStruct(shape, bf16)],
        name=f"far_backward{branches[0]}",
        aliases={len(flat) + 2 + i: i for i in range(len(before))},
        wait_for=wait_for,
    )


def column_of(plan, meta, slot):
    heads = plan.heads
    core = meta[0] if slot < heads else 1 - meta[0]
    return core * heads + slot % heads


def column_lanes(plan, meta, slot):
    return pl.ds(pl.multiple_of(column_of(plan, meta, slot) * HEAD_DIM, HEAD_DIM), HEAD_DIM)


def finish_q_body(plan, meta, off, own, got, n_own, n_got, dq, normed, mark, wide_got, sems):
    copies = []

    def send(src, dst):
        copy = pltpu.make_async_copy(src, dst, sems.at[len(copies)])
        copy.start()
        copies.append(copy)

    mine = pl.ds(pl.multiple_of(meta[0] * plan.width, plan.width), plan.width)
    send(n_own, normed.at[:, mine])
    for i in range(plan.heads):
        theirs = column_lanes(plan, meta, plan.heads + i)
        send(own.at[0, i], dq.at[:, column_lanes(plan, meta, i)])
        send(n_got.at[i], normed.at[:, theirs])
        wide_got[i] = got[i].astype(f32)
        send(wide_got.at[i], dq.at[:, theirs])
    for copy in copies:
        copy.wait()
    mark[...] = jnp.zeros_like(mark)


def finish_q(plan, own, got, n_own, n_got):
    full = (plan.rows, 2 * plan.width)
    return plan.call(
        functools.partial(finish_q_body, plan),
        [own, got, n_own, n_got],
        [
            jax.ShapeDtypeStruct(full, f32),
            jax.ShapeDtypeStruct(full, bf16),
            jax.ShapeDtypeStruct((8, HEAD_DIM), f32),
        ],
        [
            pltpu.VMEM((plan.heads, plan.rows, HEAD_DIM), f32),
            pltpu.SemaphoreType.DMA((3 * plan.heads + 1,)),
        ],
        name="finish_q",
        out_place=[pltpu.HBM, pltpu.HBM, pltpu.VMEM],
    )


def fold_body(plan, meta, off, own, got_k, got_v, sums):
    for h in range(plan.heads):
        for t, got in enumerate((got_k, got_v)):
            sums[t, h] = own[1 + t, h]
            sums[t, plan.heads + h] = got[h].astype(f32)


def fold(plan, own, got):
    shape = (2, 2 * plan.heads, plan.rows, HEAD_DIM)
    return plan.call(
        functools.partial(fold_body, plan),
        [own, *got],
        [jax.ShapeDtypeStruct(shape, f32)],
        name="fold",
    )[0]


def finish_kv_body(plan, meta, off, given, *refs):
    row_refs, (dk, dv, sums, sems) = refs[:-4], refs[-4:]
    copies = []
    for slot in range(2 * plan.heads):
        side, h = divmod(slot, plan.heads)
        for t in range(2):
            sums[t, slot] = given[t, slot]
        row = 0
        for branch in FAR:
            taken = plan.taken(branch)
            start = off[branch - 1, meta[1] + column_of(plan, meta, slot)]
            where = pl.ds(start, taken, stride=2**branch)
            for t in range(2):
                rows = row_refs[side][t, h, row : row + taken, :].astype(f32)
                sums[t, slot, where, :] = sums[t, slot, where, :] + rows
            row += taken
        for t, out in enumerate((dk, dv)):
            copy = pltpu.make_async_copy(
                sums.at[t, slot], out.at[:, column_lanes(plan, meta, slot)], sems.at[len(copies)]
            )
            copy.start()
            copies.append(copy)
    for copy in copies:
        copy.wait()


def finish_kv(plan, sums, own, got):
    full = jax.ShapeDtypeStruct((plan.rows, 2 * plan.width), f32)
    return plan.call(
        functools.partial(finish_kv_body, plan),
        [sums, own, got],
        [full, full],
        [pltpu.VMEM(sums.shape, f32), pltpu.SemaphoreType.DMA((4 * plan.heads,))],
        name="finish_kv",
        out_place=pltpu.HBM,
    )


def gather(plan, msgs, filler, last_filler=None):
    two, three, four = msgs
    four_far, three_y, three_z = flip(four, "seq", 8), flip(three, "seq", 2), flip(three, "seq", 4)
    two_y = flip(two, "seq", 2)
    both, for_z = relay(plan, three_y, four, four_far, [filler(), three_z])
    four_y, from_z = flip(both, "seq", 2), flip(for_z, "seq", 4)
    four_yz = flip(last_filler(four_y, both, two_y) if last_filler else four_y, "seq", 4)
    rows_three, rows_four = three.shape[3], four.shape[3]
    from_z_four = [Rows(from_z, rows_three + i * rows_four, rows_four) for i in range(2)]
    return (
        [whole_rows(x) for x in (two, two_y)],
        [whole_rows(x) for x in (three, three_y, three_z)] + [Rows(from_z, 0, rows_three)],
        [whole_rows(x) for x in (four, four_far, four_y)] + from_z_four + [whole_rows(four_yz)],
    )


def shards(queries, key_rows, value_rows, stream, norm_gain, norm_bias, head_offsets, cotangent):
    rows = queries.shape[0]
    heads_here = queries.shape[1] // HEAD_DIM
    half = queries.shape[1] // 2
    core = lax.axis_index("seq") & 1
    first_head = lax.axis_index("head") * heads_here
    meta = jnp.stack([core, first_head]).astype(jnp.int32)
    plan = Plan(rows, heads_here, meta, head_offsets)
    gain, bias = norm_gain[None, :], norm_bias[None, :]

    kv_sent = halves(plan, [key_rows, value_rows])
    kv_got = flip(kv_sent, "seq", 1)
    qsc_got = flip(halves(plan, [queries, stream, cotangent]), "seq", 1)
    kv_far = pick(plan, [key_rows, value_rows], kv_got, 0)
    near = near_forward(plan, queries, key_rows, value_rows, kv_got, qsc_got)
    kv_pieces = gather(plan, kv_far, lambda: near[1])
    q_far = pick(plan, [queries], qsc_got, 0)
    far = [far_forward(plan, b, q_far[b - 2], kv_pieces[b - 2]) for b in FAR]
    q_two_y = flip(q_far[0], "seq", 2)
    attn, lse, stats = combine(plan, near, far, stream, cotangent, qsc_got, gain)

    stats = join(plan, stats, flip(stats, "seq", 1), half, swap=True)
    width, mask = 4 * half, 1
    while 2 * mask < lax.axis_size("head"):
        stats = join(plan, stats, flip(stats, "head", mask), width // 2)
        width, mask = 2 * width, 2 * mask
    n_own, n_send, da, delta, *msgs = norm(
        plan,
        width,
        stats,
        flip(stats, "head", mask),
        attn,
        lse,
        stream,
        cotangent,
        qsc_got,
        gain,
        bias,
        q_far[1:],
        [q_two_y],
    )

    n_got = flip(n_send, "seq", 1)
    ins = [queries, key_rows, value_rows, kv_got, qsc_got, da, lse, delta]
    first = max(1, plan.heads // 4)
    parts = []

    def near_first():
        parts.append(near_backward(plan, 0, first, ins, kv_pieces))
        return parts[-1][0]

    def near_rest(four_y, *ready):
        own, *sends = near_backward(
            plan, first, plan.heads - first, ins, kv_pieces, parts[-1], wait_for=[*ready, n_got]
        )
        four_y, own = lax.optimization_barrier((four_y, own))
        parts.append((own, *sends))
        return four_y

    msg_pieces = gather(plan, msgs, near_first, near_rest)
    own, *sends = parts[-1]
    got_q, *got_kv = [flip(send, "seq", 1) for send in sends]
    grad_query, normed_out, mark = finish_q(plan, own, got_q, n_own, n_got)
    sums = fold(plan, own, got_kv)
    rows, done = (), [own]
    for group in GROUPS:
        low, high = group[0] - 2, group[-1] - 1
        q_two = [q_far[0], q_two_y] if group[0] == 2 else []
        rows = far_backward(plan, group, kv_far[low:high], msg_pieces[low:high], q_two, done, rows)
        done = [mark, sums]
    grad_key, grad_value = finish_kv(plan, sums, rows[0], flip(rows[1], "seq", 1))
    return normed_out, grad_query, grad_key, grad_value


def solution(mesh):
    return jax.shard_map(
        shards,
        mesh=mesh,
        in_specs=(
            P("seq", "head"),
            P("seq", "head"),
            P("seq", "head"),
            P("seq", "head"),
            P("head"),
            P("head"),
            P(),
            P("seq", "head"),
        ),
        out_specs=(P("seq", "head"), P("seq", "head"), P("seq", "head"), P("seq", "head")),
        check_vma=False,
    )
```

```python
import functools
import math
from typing import NamedTuple

import jax
import jax.numpy as jnp
from jax import lax
from jax.experimental import pallas as pl
from jax.experimental.pallas import tpu as pltpu
from jax.sharding import PartitionSpec as P

HEAD_DIM = 128
BRANCHES = 4
FAR = (2, 3, 4)
GROUPS = ((2, 3), (4,))
STAT_ROWS = 8
COPIES = 4

alpha_res = (2.0 * 24.0) ** 0.25
eps_norm = 1e-05
scaling = HEAD_DIM ** (-0.5)
scaling2 = scaling * math.log2(math.e)

f32 = jnp.float32
bf16 = jnp.bfloat16


def dot_nt(a, b):
    return lax.dot_general(a, b, (((1,), (1,)), ((), ())), preferred_element_type=f32)


def dot_nn(a, b):
    return lax.dot_general(a, b, (((1,), (0,)), ((), ())), preferred_element_type=f32)


def dot_tn(a, b):
    return lax.dot_general(a, b, (((0,), (0,)), ((), ())), preferred_element_type=f32)


def flip(block, axis, mask):
    count = lax.axis_size(axis)
    return lax.ppermute(block, axis, [(i, i ^ mask) for i in range(count)])


def wide(column_block, times):
    return jnp.concatenate([column_block] * times, axis=1)


def attended(scores, value):
    peak = jnp.max(scores, axis=1, keepdims=True)
    weights = jnp.exp2((scores - peak) * scaling2).astype(bf16)
    both = dot_nn(weights, jnp.concatenate([value, jnp.ones_like(value)], axis=1))
    total = both[:, HEAD_DIM:]
    return both[:, :HEAD_DIM] / total, peak * scaling2 + jnp.log2(total)


def attend(query, key, value):
    return attended(dot_nt(query, key), value)


def staggered(items, begin, end, depth=2):
    waiting = []
    for item in items:
        waiting.append(begin(*item))
        if len(waiting) > depth:
            end(*waiting.pop(0))
    for item in waiting:
        end(*item)


def merged(out_a, lse_a, out_b, lse_b):
    peak = jnp.maximum(lse_a, lse_b)
    part_a = jnp.exp2(lse_a - peak)
    part_b = jnp.exp2(lse_b - peak)
    total = part_a + part_b
    return (out_a * part_a + out_b * part_b) / total, peak + jnp.log2(total)


def room(scratch):
    arrays = [x for x in scratch if not isinstance(x, pltpu.SemaphoreType) and hasattr(x, "memory_space")]
    arrays = [x for x in arrays if x.memory_space == pltpu.VMEM]
    return sum(math.prod(x.shape) * jnp.dtype(x.dtype).itemsize for x in arrays) + 4 * 2**20


class Plan:
    def __init__(self, rows, heads_here, meta, offsets):
        self.rows = rows
        self.heads = heads_here // 2
        self.width = self.heads * HEAD_DIM
        self.meta = meta
        self.offsets = offsets

    def taken(self, branch):
        return self.rows >> branch

    def call(
        self,
        body,
        ins,
        outs,
        scratch=(),
        name=None,
        in_place=pltpu.VMEM,
        out_place=pltpu.VMEM,
        aliases=None,
        wait_for=(),
    ):
        given, waited = 2 + len(ins), len(wait_for)

        def without_waited(*refs):
            body(*refs[:given], *refs[given + waited :])

        scalars = pl.BlockSpec(memory_space=pltpu.SMEM)
        return pl.pallas_call(
            without_waited if waited else body,
            out_shape=outs,
            in_specs=[scalars, scalars]
            + [pl.BlockSpec(memory_space=in_place)] * len(ins)
            + [pl.BlockSpec(memory_space=pl.ANY)] * waited,
            out_specs=[
                pl.BlockSpec(memory_space=out_place[i] if isinstance(out_place, list) else out_place)
                for i in range(len(outs))
            ],
            scratch_shapes=list(scratch),
            compiler_params=pltpu.CompilerParams(vmem_limit_bytes=room(scratch)),
            cost_estimate=pl.CostEstimate(flops=0, bytes_accessed=0, transcendentals=0),
            input_output_aliases=aliases or {},
            name=name,
        )(self.meta, self.offsets, *ins, *wait_for)

    def each_head(self, together, body):
        together = min(together, self.heads)
        if together == self.heads:
            for h in range(self.heads):
                body(h, h)
            return

        def step(i, carry):
            for slot in range(together):
                body(i * together + slot, slot)
            return carry

        lax.fori_loop(0, self.heads // together, step, 0)


def head_groups(heads, together, body):
    together = min(together, heads)

    def step(i, carry):
        body([i * together + slot for slot in range(together)])
        return carry

    if together == heads:
        body(list(range(heads)))
    else:
        lax.fori_loop(0, heads // together, step, 0)


def lanes(h):
    if isinstance(h, int):
        return slice(h * HEAD_DIM, (h + 1) * HEAD_DIM)
    return pl.ds(pl.multiple_of(h * HEAD_DIM, HEAD_DIM), HEAD_DIM)


def own_lanes(meta, heads, h):
    return pl.ds(pl.multiple_of((meta[0] * heads + h) * HEAD_DIM, HEAD_DIM), HEAD_DIM)


def member_rows(meta, off, heads, branch, h, taken, shift=0):
    start = off[branch - 1, meta[1] + meta[0] * heads + h]
    return pl.ds(start + shift, taken, stride=2**branch)


def halves_body(plan, count, meta, off, *refs):
    ins, out, sems = refs[:count], refs[count], refs[count + 1]
    other = pl.ds(pl.multiple_of((1 - meta[0]) * plan.width, plan.width), plan.width)
    step = plan.rows // COPIES
    copies = []
    for i, ref in enumerate(ins):
        for j in range(COPIES):
            rows = slice(j * step, (j + 1) * step)
            sem = sems.at[i * COPIES + j]
            copies.append(pltpu.make_async_copy(ref.at[rows, other], out.at[i, rows], sem))
    for copy in copies:
        copy.start()
    for copy in copies:
        copy.wait()


def halves(plan, blocks, wait_for=()):
    count = len(blocks)
    out = jax.ShapeDtypeStruct((count, plan.rows, plan.width), blocks[0].dtype)
    return plan.call(
        functools.partial(halves_body, plan, count),
        [pltpu.with_memory_space_constraint(x, pltpu.HBM) for x in blocks],
        [out],
        [pltpu.SemaphoreType.DMA((count * COPIES,))],
        name="halves",
        wait_for=wait_for,
        in_place=pltpu.HBM,
    )[0]


def pick_body(plan, count, first, meta, off, *refs):
    owns, got, outs, scratch = refs[:count], refs[count], refs[count + 1 : count + 4], refs[-1]
    heads, rows = plan.heads, plan.rows

    def one(h, slot):
        for i in range(count):
            scratch[slot, 2 * i] = owns[i][:, own_lanes(meta, heads, h)].astype(f32)
            scratch[slot, 2 * i + 1] = got[first + i, :, lanes(h)].astype(f32)
        for branch, out in zip(FAR, outs):
            taken = plan.taken(branch)
            where = member_rows(meta, off, heads, branch, h, taken)
            for i in range(count):
                picked = [scratch[slot, 2 * i + seg, where, :] for seg in range(2)]
                out[0, i, h] = jnp.concatenate(picked, axis=0).astype(bf16)

    plan.each_head(4, one)


def pick(plan, owns, got, first):
    count = len(owns)
    outs = [
        jax.ShapeDtypeStruct((1, count, plan.heads, 2 * plan.taken(b), HEAD_DIM), bf16) for b in FAR
    ]
    return plan.call(
        functools.partial(pick_body, plan, count, first),
        [*owns, got],
        outs,
        [pltpu.VMEM((4, 2 * count, plan.rows, HEAD_DIM), f32)],
        name="pick",
    )


def near_forward_body(plan, together, meta, off, qo, ko, vo, kv_got, q_got, out, lse, wide_in, acc, acc_l):
    heads, rows, taken = plan.heads, plan.rows, plan.taken(1)

    def one(h, slot):
        mine = own_lanes(meta, heads, h)
        seg_in = (
            (qo[:, mine], ko[:, mine], vo[:, mine]),
            (q_got[0, :, lanes(h)], kv_got[0, :, lanes(h)], kv_got[1, :, lanes(h)]),
        )
        for seg in range(2):
            for i in range(3):
                wide_in[slot, 2 * i + seg] = seg_in[seg][i].astype(f32)
        where = member_rows(meta, off, heads, 1, h, taken)
        near = []
        for i in range(3):
            picked = [wide_in[slot, 2 * i + seg, where, :] for seg in range(2)]
            near.append(jnp.concatenate(picked, axis=0).astype(bf16))
        for seg in range(2):
            o, l2 = attend(*seg_in[seg])
            acc[slot, seg] = o
            acc_l[slot, seg] = l2
        o, l2 = attend(*near)
        for seg in range(2):
            part = slice(seg * taken, (seg + 1) * taken)
            new_o, new_l = merged(
                acc[slot, seg, where, :], acc_l[slot, seg, where, :], o[part], l2[part]
            )
            acc[slot, seg, where, :] = new_o
            acc_l[slot, seg, where, :] = new_l
        for seg in range(2):
            part = slice(seg * rows, (seg + 1) * rows)
            out[h, part, :] = acc[slot, seg]
            lse[h, part, :] = acc_l[slot, seg]

    plan.each_head(together, one)


def near_forward(plan, q, k, v, kv_got, q_got):
    rows, heads = plan.rows, plan.heads
    together = 2
    out = jax.ShapeDtypeStruct((heads, 2 * rows, HEAD_DIM), f32)
    pair = pltpu.VMEM((together, 2, rows, HEAD_DIM), f32)
    return plan.call(
        functools.partial(near_forward_body, plan, together),
        [q, k, v, kv_got, q_got],
        [out, out],
        [pltpu.VMEM((together, 6, rows, HEAD_DIM), f32), pair, pair],
        name="near_forward",
    )


class Rows(NamedTuple):
    array: jax.Array
    start: int
    count: int


def whole_rows(array):
    return Rows(array, 0, array.shape[3])


def extents(pieces):
    return [(p.array.shape[0], p.start, p.count) for p in pieces]


def gathered(refs, layout, which, h):
    parts = []
    for ref, (many, start, count) in zip(refs, layout, strict=True):
        for n in range(many):
            parts.append(ref[n, which, h, start : start + count, :])
    return jnp.concatenate(parts, axis=0)


def far_forward_body(plan, layout, meta, off, q, *refs):
    pieces, out, lse = refs[:-2], refs[-2], refs[-1]

    def begin(h):
        return h, dot_nt(q[0, 0, h], gathered(pieces, layout, 0, h))

    def end(h, scores):
        out[h], lse[h] = attended(scores, gathered(pieces, layout, 1, h))

    head_groups(plan.heads, 8, lambda hs: staggered([(h,) for h in hs], begin, end))


def far_forward(plan, branch, q, pieces):
    rows, heads = 2 * plan.taken(branch), plan.heads
    outs = [jax.ShapeDtypeStruct((heads, rows, HEAD_DIM), f32)] * 2
    return plan.call(
        functools.partial(far_forward_body, plan, extents(pieces)),
        [q, *[p.array for p in pieces]],
        outs,
        name=f"far_forward{branch}",
    )


def combine_body(plan, meta, off, *refs):
    near_o, near_l, far, (so, co, sc_got, gain) = refs[0], refs[1], refs[2:8], refs[8:12]
    attn, lse, stats, pre_all, g_all = refs[12:]
    rows, heads = plan.rows, plan.heads

    def one(h, slot):
        mine = own_lanes(meta, heads, h)
        attn[h] = near_o[h]
        lse[h] = near_l[h]
        for i, branch in enumerate(FAR):
            taken = plan.taken(branch)
            for seg in range(2):
                where = member_rows(meta, off, heads, branch, h, taken, seg * rows)
                part = slice(seg * taken, (seg + 1) * taken)
                new_o, new_l = merged(
                    attn[h, where, :], lse[h, where, :], far[2 * i][h, part], far[2 * i + 1][h, part]
                )
                attn[h, where, :] = new_o
                lse[h, where, :] = new_l
        scale = gain[:, mine]
        res = (so[:, mine], sc_got[1, :, lanes(h)])
        cot = (co[:, mine], sc_got[2, :, lanes(h)])
        for seg in range(2):
            part = slice(seg * rows, (seg + 1) * rows)
            pre_all[h, part, :] = alpha_res * res[seg].astype(f32) + attn[h, part, :]
            g_all[h, part, :] = cot[seg].astype(f32) * scale

    plan.each_head(2, one)

    def total(i, acc):
        return acc + pre_all[i]

    for seg in range(2):
        part = slice(seg * rows, (seg + 1) * rows)
        acc = pre_all[0, part, :]
        for i in range(1, heads):
            acc = acc + pre_all[i, part, :]
        pre_sum = jnp.sum(acc, axis=1, keepdims=True)
        centre = pre_sum / (heads * HEAD_DIM)
        second = jnp.zeros((rows, HEAD_DIM), f32)
        g_sum, cross = second, second
        for i in range(heads):
            diff = pre_all[i, part, :] - centre
            g = g_all[i, part, :]
            second, g_sum, cross = second + diff * diff, g_sum + g, cross + g * diff
        lane = lax.broadcasted_iota(jnp.int32, (rows, HEAD_DIM), 1)
        table = jnp.broadcast_to(pre_sum, (rows, HEAD_DIM))
        for i, x in enumerate((second, g_sum, cross)):
            table = jnp.where(lane == i + 1, jnp.sum(x, axis=1, keepdims=True), table)
        stats[:, part] = jnp.transpose(table)[:STAT_ROWS]


def combine(plan, near, far, stream, cot, sc_got, gain):
    rows, heads = plan.rows, plan.heads
    per_head = jax.ShapeDtypeStruct((heads, 2 * rows, HEAD_DIM), f32)
    outs = [per_head, per_head, jax.ShapeDtypeStruct((STAT_ROWS, 2 * rows), f32)]
    return plan.call(
        functools.partial(combine_body, plan),
        [*near, *[x for pair in far for x in pair], stream, cot, sc_got, gain],
        outs,
        [pltpu.VMEM((heads, 2 * rows, HEAD_DIM), f32)] * 2,
        name="combine",
    )


def joined(mine, other, count):
    gap = (mine[0:1] - other[0:1]) / count
    return [
        mine[0:1] + other[0:1],
        mine[1:2] + other[1:2] + gap * gap * (count / 2),
        mine[2:3] + other[2:3],
        mine[3:4] + other[3:4] + gap * 0.5 * (mine[2:3] - other[2:3]),
    ]


def join_body(rows, count, swap, meta, off, mine, other, out):
    theirs = other[...]
    if swap:
        theirs = jnp.concatenate([theirs[:, rows:], theirs[:, :rows]], axis=1)
    for i, row in enumerate(joined(mine[...], theirs, count)):
        out[i : i + 1, :] = row


def join(plan, mine, other, count, swap=False):
    return plan.call(
        functools.partial(join_body, plan.rows, count, swap),
        [mine, other],
        [jax.ShapeDtypeStruct(mine.shape, f32)],
        name="join",
    )[0]


def relay_body(meta, off, three, four, four_far, both, for_z):
    both[0:1] = four[...]
    both[1:2] = four_far[...]
    place = 0
    for ref in (three, four, four_far):
        rows = ref.shape[3]
        for c in range(ref.shape[1]):
            for h in range(ref.shape[2]):
                for_z[0, c, h, place : place + rows, :] = ref[0, c, h]
        place += rows


def relay(plan, three, four, four_far, wait_for):
    _, tensors, heads, rows, width = four.shape
    sd = jax.ShapeDtypeStruct
    outs = [
        sd((2, tensors, heads, rows, width), four.dtype),
        sd((1, tensors, heads, three.shape[3] + 2 * rows, width), four.dtype),
    ]
    return plan.call(relay_body, [three, four, four_far], outs, name="relay", wait_for=wait_for)


def split_rows(lse, delta):
    high = lse.astype(bf16).astype(f32)
    mid = (lse - high).astype(bf16).astype(f32)
    low = lse - high - mid
    delta_high = delta.astype(bf16).astype(f32)
    delta_low = delta - delta_high
    return jnp.concatenate(
        [high, mid, low, delta_high, delta_low] + [jnp.zeros_like(lse)] * (STAT_ROWS - 5), axis=0
    ).astype(bf16)


def norm_body(plan, full_width, together, meta, off, *refs):
    stats, stats_got, attn, lse, so, co, sc_got, gain, bias = refs[:9]
    q_far = (None, *refs[9:11])
    n_own, n_send, da_out, delta_out, m2, m3, m4, cols, da_wide, delta_wide = refs[11:]
    rows, heads = plan.rows, plan.heads
    st = joined(stats[...], stats_got[...], full_width // 2)
    centre = st[0] / full_width
    inv = 1.0 / jnp.sqrt(st[1] / full_width + eps_norm)
    for i, row in enumerate((centre, inv, st[2] / full_width, st[3] * inv / full_width)):
        cols[i] = jnp.transpose(jnp.broadcast_to(row, (HEAD_DIM, 2 * rows)))

    def one(h, slot):
        mine = own_lanes(meta, heads, h)
        scale, shift = gain[:, mine], bias[:, mine]
        res = (so[:, mine], sc_got[1, :, lanes(h)])
        cot = (co[:, mine], sc_got[2, :, lanes(h)])
        for seg in range(2):
            part = slice(seg * rows, (seg + 1) * rows)
            att = attn[h, part, :]
            inv_col = cols[1, part, :]
            normed = (alpha_res * res[seg].astype(f32) + att - cols[0, part, :]) * inv_col
            if seg == 0:
                n_own[:, lanes(h)] = (scale * normed + shift).astype(bf16)
            else:
                n_send[h] = (scale * normed + shift).astype(bf16)
            g = cot[seg].astype(f32) * scale
            da = (inv_col * (g - cols[2, part, :] - normed * cols[3, part, :])).astype(bf16)
            da_out[h, part, :] = da
            da_f = da.astype(f32)
            da_wide[slot, part, :] = da_f
            delta = jnp.broadcast_to(jnp.sum(da_f * att, axis=1, keepdims=True), (rows, HEAD_DIM))
            delta_wide[slot, part, :] = delta
            delta_out[h, part, :] = delta
        for branch, msg, q_rows in zip(FAR, (m2, m3, m4), q_far):
            taken = plan.taken(branch)
            where = [member_rows(meta, off, heads, branch, h, taken, seg * rows) for seg in range(2)]
            picked = jnp.concatenate([da_wide[slot, w, :] for w in where], axis=0)
            msg[0, 0, h, : 2 * taken, :] = picked.astype(bf16)
            pad = [jnp.zeros((HEAD_DIM - 2 * taken, HEAD_DIM), f32)] if 2 * taken < HEAD_DIM else []
            lse_rows = jnp.concatenate([lse[h, w, :] for w in where] + pad, axis=0)
            delta_rows = jnp.concatenate([delta_wide[slot, w, :] for w in where] + pad, axis=0)
            if q_rows is not None:
                msg[0, 0, h, 2 * taken + STAT_ROWS :, :] = q_rows[0, 0, h]
            msg[0, 0, h, 2 * taken : 2 * taken + STAT_ROWS, :] = split_rows(
                jnp.transpose(lse_rows)[0:1], jnp.transpose(delta_rows)[0:1]
            )

    plan.each_head(together, one)


def norm(plan, full_width, stats, stats_got, attn, lse, stream, cot, sc_got, gain, bias, q_far, wait_for):
    rows, heads = plan.rows, plan.heads
    sd = jax.ShapeDtypeStruct
    together = 2
    outs = [
        sd((rows, plan.width), bf16),
        sd((heads, rows, HEAD_DIM), bf16),
        sd((heads, 2 * rows, HEAD_DIM), bf16),
        sd((heads, 2 * rows, HEAD_DIM), f32),
    ] + [sd((1, 1, heads, (2 if b == 2 else 4) * plan.taken(b) + STAT_ROWS, HEAD_DIM), bf16) for b in FAR]
    wide_rows = pltpu.VMEM((together, 2 * rows, HEAD_DIM), f32)
    return plan.call(
        functools.partial(norm_body, plan, full_width, together),
        [stats, stats_got, attn, lse, stream, cot, sc_got, gain, bias, *q_far],
        outs,
        [pltpu.VMEM((4, 2 * rows, HEAD_DIM), f32), wide_rows, wide_rows],
        name="norm",
        wait_for=wait_for,
    )


def probs_and_ds(scores, dprob, lse, delta):
    reach = scores.shape[1] // HEAD_DIM
    probs = jnp.exp2(scores * scaling2 - wide(lse, reach))
    return probs.astype(bf16), (probs * (dprob - wide(delta, reach))).astype(bf16)


def near_backward_body(plan, layouts, first_head, count, meta, off, *refs):
    counts = [len(x) for x in layouts]
    qo, ko, vo, kv_got, q_got, da, lse, delta = refs[:8]
    pieces = refs[8 : 8 + sum(counts)]
    own, *sends, wide_in, sums = refs[-6:]
    rows, heads = plan.rows, plan.heads

    def load(h, slot):
        mine = own_lanes(meta, heads, h)
        seg_in = (
            (qo[:, mine], ko[:, mine], vo[:, mine], da[h, :rows, :]),
            (q_got[0, :, lanes(h)], kv_got[0, :, lanes(h)], kv_got[1, :, lanes(h)], da[h, rows:, :]),
        )
        for seg in range(2):
            for t in range(4):
                wide_in[slot, 2 * t + seg] = seg_in[seg][t].astype(f32)
        return seg_in

    def begin(h, slot, seg_in, branch, seg):
        if branch == 0:
            query, key, value, grad = seg_in[seg]
        else:
            inside = member_rows(meta, off, heads, branch, h, plan.taken(branch))

            def member(t):
                picked = [wide_in[slot, 2 * t + s, inside, :] for s in range(2)]
                return jnp.concatenate(picked, axis=0).astype(bf16)

            query, grad = member(0), member(3)
            if branch == 1:
                key, value = member(1), member(2)
            else:
                first, layout = sum(counts[: branch - 2]), layouts[branch - 2]
                far = pieces[first : first + counts[branch - 2]]
                key, value = gathered(far, layout, 0, h), gathered(far, layout, 1, h)
        return (h, slot, branch, seg, query, key, grad, dot_nt(query, key), dot_nt(grad, value))

    def end(h, slot, branch, seg, query, key, grad, scores, dprob):
        taken = plan.taken(branch)
        if branch == 0:
            where = [slice(seg * rows, (seg + 1) * rows)]
        else:
            where = [member_rows(meta, off, heads, branch, h, taken, s * rows) for s in range(2)]
        lse_rows = jnp.concatenate([lse[h, w, :] for w in where], axis=0)
        delta_rows = jnp.concatenate([delta[h, w, :] for w in where], axis=0)
        probs, ds = probs_and_ds(scores, dprob, lse_rows, delta_rows)
        grads = [dot_nn(ds, key)]
        if branch <= 1:
            grads += [dot_tn(ds, query), dot_tn(probs, grad)]
        for t, rows_new in enumerate(grads):
            for s, w in enumerate(where):
                part = rows_new[s * taken : (s + 1) * taken]
                sums[slot, t, w, :] = part if branch == 0 else sums[slot, t, w, :] + part

    def store(h, slot):
        for t, scale in enumerate((scaling, scaling, None)):
            both = sums[slot, t]
            both = both if scale is None else both * scale
            own[t, h] = both[:rows]
            sends[t][h] = both[rows:].astype(bf16)

    together = min(2, count)
    order = [(0, 0), (0, 1)] + [(branch, 0) for branch in range(1, BRANCHES + 1)]

    def step(i, carry):
        hs = [first_head + i * together + slot for slot in range(together)]
        seg_ins = [load(h, slot) for slot, h in enumerate(hs)]
        waiting = []
        for branch, seg in order:
            for slot, h in enumerate(hs):
                waiting.append(begin(h, slot, seg_ins[slot], branch, seg))
                if len(waiting) > 2:
                    end(*waiting.pop(0))
        for item in waiting:
            end(*item)
        for slot, h in enumerate(hs):
            store(h, slot)
        return carry

    lax.fori_loop(0, count // together, step, 0)


def near_backward(plan, first_head, count, ins, pieces, before=(), wait_for=()):
    shape = (plan.heads, plan.rows, HEAD_DIM)
    flat = [*ins, *[x.array for p in pieces for x in p]]
    return plan.call(
        functools.partial(near_backward_body, plan, [extents(p) for p in pieces], first_head, count),
        [*flat, *before],
        [jax.ShapeDtypeStruct((3, *shape), f32)] + [jax.ShapeDtypeStruct(shape, bf16)] * 3,
        [pltpu.VMEM((2, 8, plan.rows, HEAD_DIM), f32), pltpu.VMEM((2, 3, 2 * plan.rows, HEAD_DIM), f32)],
        name=f"near_backward{first_head}",
        aliases={len(flat) + 2 + i: i for i in range(len(before))},
        wait_for=wait_for,
    )


def far_backward_body(plan, branches, layouts, first_row, meta, off, *refs):
    counts = [len(x) for x in layouts]
    kvs, msgs, (own, send) = refs[: len(branches)], refs[len(branches) : -2], refs[-2:]
    msgs, q_two = msgs[: sum(counts)], msgs[sum(counts) : sum(counts) + 2]

    def begin(h, j, branch):
        taken = plan.taken(branch)
        grads, queries, halves_of = [], [], [None] * (plan.rows // HEAD_DIM)
        place = 0
        mine = msgs[sum(counts[:j]) : sum(counts[: j + 1])]
        for ref, (many, start, _) in zip(mine, layouts[j], strict=True):
            table_at = start + 2 * taken
            for n in range(many):
                grads.append(ref[n, 0, h, start:table_at, :])
                if branch != 2:
                    queries.append(ref[n, 0, h, table_at + STAT_ROWS : table_at + STAT_ROWS + 2 * taken, :])
                terms = ref[n, 0, h, table_at : table_at + STAT_ROWS, :].astype(f32)
                half, shift = divmod(place, HEAD_DIM)
                if shift:
                    terms = pltpu.roll(terms, shift, 1)
                halves_of[half] = terms if halves_of[half] is None else halves_of[half] + terms
                place += 2 * taken
        if branch == 2:
            queries = [ref[0, 0, h] for ref in q_two]
        grad = jnp.concatenate(grads, axis=0)
        query = jnp.concatenate(queries, axis=0)
        table = jnp.concatenate(halves_of, axis=1)
        lse = table[0:1] + table[1:2] + table[2:3]
        delta = table[3:4] + table[4:5]
        key, value = kvs[j][0, 0, h], kvs[j][0, 1, h]
        return h, branch, query, grad, lse, delta, dot_nt(key, query), dot_nt(value, grad)

    def end(h, branch, query, grad, lse, delta, scores, dprob):
        taken = plan.taken(branch)
        row = first_row + sum(plan.taken(b) for b in branches if b < branch)
        probs = jnp.exp2(scores * scaling2 - lse)
        ds = (probs * (dprob - delta)).astype(bf16)
        dkey = dot_nn(ds, query) * scaling
        dvalue = dot_nn(probs.astype(bf16), grad)
        for i, rows in enumerate((dkey, dvalue)):
            own[i, h, row : row + taken, :] = rows[:taken]
            send[i, h, row : row + taken, :] = rows[taken:].astype(bf16)

    def group(hs):
        staggered([(h, j, b) for j, b in enumerate(branches) for h in hs], begin, end)

    head_groups(plan.heads, 4, group)


def far_backward(plan, branches, kvs, pieces, q_two, wait_for, before=()):
    shape = (2, plan.heads, sum(plan.taken(b) for b in FAR), HEAD_DIM)
    first_row = sum(plan.taken(b) for b in FAR if b < branches[0])
    flat = [*kvs, *[x.array for p in pieces for x in p], *q_two]
    return plan.call(
        functools.partial(far_backward_body, plan, branches, [extents(p) for p in pieces], first_row),
        [*flat, *before],
        [jax.ShapeDtypeStruct(shape, f32), jax.ShapeDtypeStruct(shape, bf16)],
        name=f"far_backward{branches[0]}",
        aliases={len(flat) + 2 + i: i for i in range(len(before))},
        wait_for=wait_for,
    )


def column_of(plan, meta, slot):
    heads = plan.heads
    core = meta[0] if slot < heads else 1 - meta[0]
    return core * heads + slot % heads


def column_lanes(plan, meta, slot):
    return pl.ds(pl.multiple_of(column_of(plan, meta, slot) * HEAD_DIM, HEAD_DIM), HEAD_DIM)


def finish_q_body(plan, meta, off, own, got, n_own, n_got, dq, normed, mark, wide_got, sems):
    copies = []

    def send(src, dst):
        copy = pltpu.make_async_copy(src, dst, sems.at[len(copies)])
        copy.start()
        copies.append(copy)

    mine = pl.ds(pl.multiple_of(meta[0] * plan.width, plan.width), plan.width)
    send(n_own, normed.at[:, mine])
    for i in range(plan.heads):
        theirs = column_lanes(plan, meta, plan.heads + i)
        send(own.at[0, i], dq.at[:, column_lanes(plan, meta, i)])
        send(n_got.at[i], normed.at[:, theirs])
        wide_got[i] = got[i].astype(f32)
        send(wide_got.at[i], dq.at[:, theirs])
    for copy in copies:
        copy.wait()
    mark[...] = jnp.zeros_like(mark)


def finish_q(plan, own, got, n_own, n_got):
    full = (plan.rows, 2 * plan.width)
    return plan.call(
        functools.partial(finish_q_body, plan),
        [own, got, n_own, n_got],
        [
            jax.ShapeDtypeStruct(full, f32),
            jax.ShapeDtypeStruct(full, bf16),
            jax.ShapeDtypeStruct((8, HEAD_DIM), f32),
        ],
        [
            pltpu.VMEM((plan.heads, plan.rows, HEAD_DIM), f32),
            pltpu.SemaphoreType.DMA((3 * plan.heads + 1,)),
        ],
        name="finish_q",
        out_place=[pltpu.HBM, pltpu.HBM, pltpu.VMEM],
    )


def fold_body(plan, meta, off, own, got_k, got_v, sums):
    for h in range(plan.heads):
        for t, got in enumerate((got_k, got_v)):
            sums[t, h] = own[1 + t, h]
            sums[t, plan.heads + h] = got[h].astype(f32)


def fold(plan, own, got):
    shape = (2, 2 * plan.heads, plan.rows, HEAD_DIM)
    return plan.call(
        functools.partial(fold_body, plan),
        [own, *got],
        [jax.ShapeDtypeStruct(shape, f32)],
        name="fold",
    )[0]


def finish_kv_body(plan, meta, off, given, *refs):
    row_refs, (dk, dv, sums, sems) = refs[:-4], refs[-4:]
    copies = []
    for slot in range(2 * plan.heads):
        side, h = divmod(slot, plan.heads)
        for t in range(2):
            sums[t, slot] = given[t, slot]
        row = 0
        for branch in FAR:
            taken = plan.taken(branch)
            start = off[branch - 1, meta[1] + column_of(plan, meta, slot)]
            where = pl.ds(start, taken, stride=2**branch)
            for t in range(2):
                rows = row_refs[side][t, h, row : row + taken, :].astype(f32)
                sums[t, slot, where, :] = sums[t, slot, where, :] + rows
            row += taken
        for t, out in enumerate((dk, dv)):
            copy = pltpu.make_async_copy(
                sums.at[t, slot], out.at[:, column_lanes(plan, meta, slot)], sems.at[len(copies)]
            )
            copy.start()
            copies.append(copy)
    for copy in copies:
        copy.wait()


def finish_kv(plan, sums, own, got):
    full = jax.ShapeDtypeStruct((plan.rows, 2 * plan.width), f32)
    return plan.call(
        functools.partial(finish_kv_body, plan),
        [sums, own, got],
        [full, full],
        [pltpu.VMEM(sums.shape, f32), pltpu.SemaphoreType.DMA((4 * plan.heads,))],
        name="finish_kv",
        out_place=pltpu.HBM,
    )


def gather(plan, msgs, filler, last_filler=None):
    two, three, four = msgs
    four_far, three_y, three_z = flip(four, "seq", 8), flip(three, "seq", 2), flip(three, "seq", 4)
    two_y = flip(two, "seq", 2)
    both, for_z = relay(plan, three_y, four, four_far, [filler(), three_z])
    four_y, from_z = flip(both, "seq", 2), flip(for_z, "seq", 4)
    four_yz = flip(last_filler(four_y, both, two_y) if last_filler else four_y, "seq", 4)
    rows_three, rows_four = three.shape[3], four.shape[3]
    from_z_four = [Rows(from_z, rows_three + i * rows_four, rows_four) for i in range(2)]
    return (
        [whole_rows(x) for x in (two, two_y)],
        [whole_rows(x) for x in (three, three_y, three_z)] + [Rows(from_z, 0, rows_three)],
        [whole_rows(x) for x in (four, four_far, four_y)] + from_z_four + [whole_rows(four_yz)],
    )


def shards(queries, key_rows, value_rows, stream, norm_gain, norm_bias, head_offsets, cotangent):
    rows = queries.shape[0]
    heads_here = queries.shape[1] // HEAD_DIM
    half = queries.shape[1] // 2
    core = lax.axis_index("seq") & 1
    first_head = lax.axis_index("head") * heads_here
    meta = jnp.stack([core, first_head]).astype(jnp.int32)
    plan = Plan(rows, heads_here, meta, head_offsets)
    gain, bias = norm_gain[None, :], norm_bias[None, :]

    kv_sent = halves(plan, [key_rows, value_rows])
    kv_got = flip(kv_sent, "seq", 1)
    qsc_got = flip(halves(plan, [queries, stream, cotangent]), "seq", 1)
    kv_far = pick(plan, [key_rows, value_rows], kv_got, 0)
    near = near_forward(plan, queries, key_rows, value_rows, kv_got, qsc_got)
    kv_pieces = gather(plan, kv_far, lambda: near[1])
    q_far = pick(plan, [queries], qsc_got, 0)
    far = [far_forward(plan, b, q_far[b - 2], kv_pieces[b - 2]) for b in FAR]
    q_two_y = flip(q_far[0], "seq", 2)
    attn, lse, stats = combine(plan, near, far, stream, cotangent, qsc_got, gain)

    stats = join(plan, stats, flip(stats, "seq", 1), half, swap=True)
    width, mask = 4 * half, 1
    while 2 * mask < lax.axis_size("head"):
        stats = join(plan, stats, flip(stats, "head", mask), width // 2)
        width, mask = 2 * width, 2 * mask
    n_own, n_send, da, delta, *msgs = norm(
        plan,
        width,
        stats,
        flip(stats, "head", mask),
        attn,
        lse,
        stream,
        cotangent,
        qsc_got,
        gain,
        bias,
        q_far[1:],
        [q_two_y],
    )

    n_got = flip(n_send, "seq", 1)
    ins = [queries, key_rows, value_rows, kv_got, qsc_got, da, lse, delta]
    first = max(1, plan.heads // 4)
    parts = []

    def near_first():
        parts.append(near_backward(plan, 0, first, ins, kv_pieces))
        return parts[-1][0]

    def near_rest(four_y, *ready):
        own, *sends = near_backward(
            plan, first, plan.heads - first, ins, kv_pieces, parts[-1], wait_for=[*ready, n_got]
        )
        four_y, own = lax.optimization_barrier((four_y, own))
        parts.append((own, *sends))
        return four_y

    msg_pieces = gather(plan, msgs, near_first, near_rest)
    own, *sends = parts[-1]
    got_q, *got_kv = [flip(send, "seq", 1) for send in sends]
    grad_query, normed_out, mark = finish_q(plan, own, got_q, n_own, n_got)
    sums = fold(plan, own, got_kv)
    rows, done = (), [own]
    for group in GROUPS:
        low, high = group[0] - 2, group[-1] - 1
        q_two = [q_far[0], q_two_y] if group[0] == 2 else []
        rows = far_backward(plan, group, kv_far[low:high], msg_pieces[low:high], q_two, done, rows)
        done = [mark, sums]
    grad_key, grad_value = finish_kv(plan, sums, rows[0], flip(rows[1], "seq", 1))
    return normed_out, grad_query, grad_key, grad_value


def solution(mesh):
    return jax.shard_map(
        shards,
        mesh=mesh,
        in_specs=(
            P("seq", "head"),
            P("seq", "head"),
            P("seq", "head"),
            P("seq", "head"),
            P("head"),
            P("head"),
            P(),
            P("seq", "head"),
        ),
        out_specs=(P("seq", "head"), P("seq", "head"), P("seq", "head"), P("seq", "head")),
        check_vma=False,
    )
```
